32 devices in a mesh: rows: 8 (over z, x), ch: 4 (over y, core).
Axes of the slice: x: 2, y: 2, z: 4, core: 2. Of those that a mesh axis runs over, the one named last changes fastest.
Arguments:
- hidden_in: bfloat16 [2048, 512], P('rows', 'ch'), may hold values from -6 to 6
- lengths: int32 [3], replicated, may hold values from 772 to 1024, as said below
- norm_gain: float32 [256], replicated, may hold values from 0.5 to 1.5
- in_weight: bfloat16 [2, 256, 512], P(None, None, 'ch'), may hold values from -0.375 to 0.375
- conv_weight: float32 [2, 4, 512], P(None, None, 'ch'), may hold values from -3 to 3
- conv_bias: float32 [2, 512], P(None, 'ch'), may hold values from -2 to 2
- select_weight: bfloat16 [2, 512, 48], P(None, 'ch'), may hold values from -0.25 to 0.25
- step_weight: bfloat16 [2, 16, 512], P(None, None, 'ch'), may hold values from -1.5 to 1.5
- step_bias: float32 [2, 512], P(None, 'ch'), may hold values from -7 to -2
- decay_log: float32 [2, 16, 512], P(None, None, 'ch'), may hold values from -9 to 1
- skip_gain: float32 [2, 512], P(None, 'ch'), may hold values from 0.5 to 1.5
- out_weight: bfloat16 [512, 256], P('ch'), may hold values from -0.25 to 0.25
- cotangent: bfloat16 [2048, 512], P('rows', 'ch'), may hold values from -6 to 6
Outputs:
- result: bfloat16 [2048, 512], P('rows', 'ch')
- input_grad: float32 [2048, 512], P('rows', 'ch')
- gain_grad: float32 [256], replicated
- in_weight_grad: float32 [2, 256, 512], P(None, None, 'ch')
- conv_weight_grad: float32 [2, 4, 512], P(None, None, 'ch')
- conv_bias_grad: float32 [2, 512], P(None, 'ch')
- select_weight_grad: float32 [2, 512, 48], P(None, 'ch')
- step_weight_grad: float32 [2, 16, 512], P(None, None, 'ch')
- step_bias_grad: float32 [2, 512], P(None, 'ch')
- decay_log_grad: float32 [2, 16, 512], P(None, None, 'ch')
- skip_gain_grad: float32 [2, 512], P(None, 'ch')
- out_weight_grad: float32 [512, 256], P('ch')
The draws below stay inside these ranges and needn't reach their ends.
Inputs may be any that keep to these rules, and one draw needn't show every extreme that they name: `lengths`: some window has exactly 1024 valid positions in every draw.
All inputs are finite; a program needn't handle non-finite values.
Results may differ from the reference program's by a relative error of at most 0.0087.
Values may be sent and summed in bfloat16 or wider, within the bound.
No kernel may reach another device: no remote copies, remote signals or barrier semaphores. Data moves between devices by JAX's collectives and lax.ppermute only.
A program may use at most 192 MiB of HBM per device.

```python
import jax
import jax.numpy as jnp
from jax import lax

D = 256
E = 512
N = 16
R = 16
KW = 4
TOK_DEV = 256
TOKENS = 2048
WIN = 1024
WINDOWS = 3


def draw_lengths(key, part):
    first_key, second_key = jax.random.split(jax.random.fold_in(key, 17))
    drawn = jax.random.randint(first_key, (WINDOWS,), WIN // 2 + TOK_DEV + KW, WIN + 1)
    chosen = jax.random.randint(second_key, (), 0, WINDOWS)
    return jnp.where(jnp.arange(WINDOWS) == chosen, WIN, drawn).astype(jnp.int32)


def shard_levels(rng, extent, shards, low, largest):
    def one(axis_at, parts):
        draws = jax.random.uniform(jax.random.fold_in(jax.random.fold_in(rng, 6), axis_at), (parts,), jnp.float32, low / len(shards), largest / len(shards))
        return jnp.repeat(jnp.exp(draws), extent[axis_at] // parts).reshape((-1,) + (1,) * (len(extent) - axis_at - 1))

    factor_of = one(*shards[0])
    for cut in shards[1:]:
        factor_of = factor_of * one(*cut)
    return factor_of


def centred(key, shape, scale, bound, cuts=(), kind=jnp.bfloat16):
    array = scale * jax.random.normal(key, shape, jnp.float32)
    if cuts:
        array = array * shard_levels(key, shape, cuts, -0.22, 0.18)
    return jnp.clip(array, -bound, bound).astype(kind)


def setup_inputs(seed: int = 0) -> dict:
    key_list = jax.random.split(jax.random.key(seed), 14)
    hidden_in = centred(key_list[0], (TOKENS, 2 * D), 1.0, 6.0, ((0, 8), (1, 4)))
    lengths = draw_lengths(jax.random.fold_in(key_list[13], 71), 0)
    norm_gain = jnp.clip(1.0 + 0.1 * jax.random.normal(key_list[2], (D,), jnp.float32), 0.5, 1.5)
    in_weight = centred(key_list[3], (2, D, E), D ** -0.5, 0.375, ((2, 4),))
    conv_weight = centred(key_list[4], (2, KW, E), 0.5, 3.0, ((2, 4),), jnp.float32)
    conv_bias = centred(key_list[5], (2, E), 0.3, 2.0, ((1, 4),), jnp.float32)
    select_weight = centred(key_list[6], (2, E, R + 2 * N), E ** -0.5, 0.25, ((1, 4),))
    step_weight = centred(key_list[7], (2, R, E), R ** -0.5, 1.5, ((2, 4),))
    step_bias = jnp.clip(-7.0 + 5.0 * jax.random.uniform(key_list[8], (2, E), jnp.float32) ** shard_levels(key_list[8], (2, E), ((1, 4),), -0.2, 0.2), -7.0, -2.0)
    decay_log = jnp.clip(-9.0 + 10.0 * jax.random.uniform(key_list[9], (2, N, E), jnp.float32) ** shard_levels(key_list[9], (2, N, E), ((2, 4),), -0.2, 0.2), -9.0, 1.0)
    skip_gain = jnp.clip(0.5 + 1.0 * jax.random.uniform(key_list[10], (2, E), jnp.float32) ** shard_levels(key_list[10], (2, E), ((1, 4),), -0.2, 0.2), 0.5, 1.5)
    out_weight = centred(key_list[11], (E, D), E ** -0.5, 0.25, ((0, 4),))
    cotangent = centred(key_list[12], (TOKENS, 2 * D), 1.0, 6.0, ((0, 8), (1, 4)))
    return {"hidden_in": hidden_in, "lengths": lengths, "norm_gain": norm_gain, "in_weight": in_weight, "conv_weight": conv_weight, "conv_bias": conv_bias, "select_weight": select_weight, "step_weight": step_weight, "step_bias": step_bias, "decay_log": decay_log, "skip_gain": skip_gain, "out_weight": out_weight, "cotangent": cotangent}


@jax.custom_vjp
def low(v):
    return lax.optimization_barrier(v.astype(jnp.bfloat16)).astype(jnp.float32)

@jax.custom_vjp
def low_back(v):
    return v

def low_keep(v):
    return (low(v), None)

def low_pass(kept, grad):
    return (grad,)

def back_keep(v):
    return (v, None)

def back_low(kept, grad):
    return (low(grad),)
low.defvjp(low_keep, low_pass)
low_back.defvjp(back_keep, back_low)
epsilon = 1e-06

def matmul(left, right):
    return jnp.dot(left, right, precision=lax.Precision.HIGHEST, preferred_element_type=jnp.float32)

def rms_scale(source):
    return source * lax.rsqrt(lax.optimization_barrier(jnp.mean(source * source, axis=-1, keepdims=True)) + epsilon)

def conv_causal(inputs, weight, bias_row):
    taps = weight.shape[0]
    padded = jnp.concatenate([jnp.zeros((taps - 1, inputs.shape[1]), jnp.float32), inputs], axis=0)
    running = jnp.zeros(inputs.shape, jnp.float32) + bias_row[None, :]
    for offset in range(taps):
        running = running + weight[offset][None, :] * padded[offset:offset + inputs.shape[0]]
    return running

def selective(step_row, input_row, write_row, read_row, a_matrix):

    def advance(carried, pieces):
        step_one, input_one, write_one, read_one = pieces
        carried = jnp.exp(step_one[None, :] * a_matrix) * carried + write_one[:, None] * (step_one * input_one)[None, :]
        return (carried, lax.optimization_barrier(jnp.sum(read_one[:, None] * carried, axis=0)))
    anchor = jnp.zeros(a_matrix.shape, jnp.float32)
    _, outputs = lax.scan(jax.checkpoint(advance), anchor, (step_row, input_row, write_row, read_row))
    return outputs

def mixer_local(inputs, gate_in, valid_rows, weights, course, reverse):
    conv_weight, conv_bias, select_weight, step_weight, step_bias, decay_log, skip_gain = weights
    if reverse:
        inputs, gate_in, valid_rows = (inputs[::-1], gate_in[::-1], valid_rows[::-1])
    activated = low(jax.nn.silu(conv_causal(inputs, conv_weight[course], conv_bias[course])))
    projected = low_back(matmul(activated, select_weight[course]))
    step_in = low(projected[:, :R])
    step_raw = low_back(matmul(step_in, step_weight[course]) + step_bias[course][None, :])
    step_row = jax.nn.softplus(step_raw) * valid_rows[:, None]
    write_row = projected[:, R:R + N]
    read_row = projected[:, R + N:]
    a_matrix = -jnp.exp(decay_log[course])
    outcome = selective(step_row, activated, write_row, read_row, a_matrix) + skip_gain[course][None, :] * activated
    outcome = outcome * jax.nn.silu(gate_in)
    if reverse:
        outcome = outcome[::-1]
    return outcome

def window_layer(rows_in, valid_rows, gain, in_weight, out_weight, weights):
    sources = (rows_in[:, :D], rows_in[:, D:][:, ::-1])
    branches = []
    for strand in range(2):
        normed = low(rms_scale(sources[strand]) * gain[None, :])
        inputs = low(low_back(matmul(normed, in_weight[0]) * valid_rows[:, None]))
        gate_in = low_back(matmul(normed, in_weight[1]))
        first_out = mixer_local(inputs, gate_in, valid_rows, weights, 0, strand == 1)
        second_out = mixer_local(inputs, gate_in, valid_rows, weights, 1, strand == 0)
        mixed = low((first_out + second_out) * valid_rows[:, None])
        branches.append(matmul(mixed, out_weight))
    return rows_in + jnp.concatenate([branches[0], branches[1][:, ::-1]], axis=1)

def reference(hidden_in, lengths, norm_gain, in_weight, conv_weight, conv_bias, select_weight, step_weight, step_bias, decay_log, skip_gain, out_weight, cotangent):
    half_win = WIN // 2
    position = jnp.arange(WIN, dtype=jnp.int32)
    global_pos = jnp.arange(WINDOWS, dtype=jnp.int32)[:, None] * WIN + position[None, :]
    real_rows = (global_pos >= half_win) & (global_pos < half_win + TOKENS)
    valid_all = ((position[None, :] < lengths[:, None]) & real_rows).astype(jnp.float32)

    def forward(rows_in, gain, in_w, conv_w, conv_b, select_w, step_w, step_b, decay_w, skip_w, out_w):
        weights = (conv_w, conv_b, select_w, step_w, step_b, decay_w, skip_w)
        filler = jnp.zeros((half_win, 2 * D), jnp.float32)
        extended = jnp.concatenate([filler, rows_in, filler], axis=0)
        windows = extended.reshape(WINDOWS, WIN, 2 * D)

        def one_window(rows_one, valid_one):
            return window_layer(rows_one, valid_one, gain, in_w, out_w, weights)
        outcome = jax.vmap(one_window)(windows, valid_all)
        return outcome.reshape(WINDOWS * WIN, 2 * D)[half_win:half_win + TOKENS]
    floats = (hidden_in.astype(jnp.float32), norm_gain, in_weight.astype(jnp.float32), conv_weight, conv_bias, select_weight.astype(jnp.float32), step_weight.astype(jnp.float32), step_bias, decay_log, skip_gain, out_weight.astype(jnp.float32))
    outcome, pull_back = jax.vjp(forward, *floats)
    grads = pull_back(cotangent.astype(jnp.float32))
    return (outcome.astype(jnp.bfloat16), grads[0], grads[1], grads[2], grads[3], grads[4], grads[5], grads[6], grads[7], grads[8], grads[9], grads[10])
```

```python
import functools

import jax
import jax.numpy as jnp
from jax import lax
from jax.experimental import pallas as pl
from jax.experimental.pallas import tpu as pltpu
from jax.sharding import PartitionSpec as P

N = 16
R = 16
WINDOW = 16384
LANES = 128
CHUNKS = 8
EPSILON = 1e-06
LOG2E = 1.4426950408889634
F32 = jnp.float32
BF16 = jnp.bfloat16
VM = pl.BlockSpec(memory_space=pltpu.VMEM)
SM = pl.BlockSpec(memory_space=pltpu.SMEM)
FLIPS = (False, True, True, False)


def nn(left, right):
    return lax.dot_general(left, right, (((1,), (0,)), ((), ())), preferred_element_type=F32)


def nt(left, right):
    return lax.dot_general(left, right, (((1,), (1,)), ((), ())), preferred_element_type=F32)


def tn(left, right):
    return lax.dot_general(left, right, (((0,), (0,)), ((), ())), preferred_element_type=F32)


def iota(shape, dim):
    return lax.broadcasted_iota(jnp.int32, shape, dim)


def one_hot(mask):
    return jnp.where(mask, 1.0, 0.0).astype(BF16)


def permuter(tok):
    steps = tok // CHUNKS
    row, col = iota((tok, tok), 0), iota((tok, tok), 1)
    return one_hot((row % CHUNKS) * steps + row // CHUNKS == col)


def unpermuter(tok):
    steps = tok // CHUNKS
    row, col = iota((tok, tok), 0), iota((tok, tok), 1)
    return one_hot((col % CHUNKS) * steps + col // CHUNKS == row)


def mirror(width):
    return one_hot(iota((width, width), 0) + iota((width, width), 1) == width - 1)


def sigmoid(v):
    return 1.0 / (1.0 + jnp.exp(-v))


def silu(v):
    return v * sigmoid(v)


def silu_slope(v):
    logistic = sigmoid(v)
    return logistic * (1.0 + v * (1.0 - logistic))


def softplus(v):
    return jnp.maximum(v, 0.0) + jnp.log1p(jnp.exp(-jnp.abs(v)))


def low(v):
    return v.astype(BF16)


class Geometry:
    def __init__(self, tok, rows):
        self.tok = tok
        self.rows = rows
        self.window = min(WINDOW, tok * rows // 2)
        self.members = self.window // tok
        self.steps = tok // CHUNKS

    def place(self, lengths_ref):
        row = lax.axis_index("rows")
        shifted = row * self.tok + self.window // 2
        offset = lax.rem(shifted, self.window)
        length = lengths_ref[lax.div(shifted, self.window)]
        return row, offset, length

    def valid(self, lengths_ref):
        _, offset, length = self.place(lengths_ref)
        row = iota((self.tok, 1), 0)
        token = (row % CHUNKS) * self.steps + row // CHUNKS
        return jnp.where(offset + token < length, 1.0, 0.0)

    def local(self):
        row = lax.axis_index("rows")
        return lax.rem(row + self.members // 2, self.members)

    def near(self):
        return [(i, i ^ 1) for i in range(self.rows)]

    def far(self):
        if self.members == 4:
            return self.swaps(lambda k: 3 - k)
        out = []
        for i in range(1, self.rows, 2):
            out += [(i, (i + 1) % self.rows), ((i + 1) % self.rows, i)]
        return out

    def across(self):
        return self.swaps(lambda k: (k + 2) % 4)

    def swaps(self, other):
        out = []
        for i in range(self.rows):
            local = (i + 2) % 4
            j = i - local + other(local)
            out.append((i, j if 0 <= j < self.rows else i ^ 1))
        return out


def run(kernel, outs, *args, smem=0, scratch=(), name=None, cost=None):
    single = isinstance(outs, tuple)
    shapes = [outs] if single else list(outs)
    got = pl.pallas_call(
        kernel,
        out_shape=[jax.ShapeDtypeStruct(s, d) for s, d in shapes],
        in_specs=[SM] * smem + [VM] * (len(args) - smem),
        out_specs=[VM] * len(shapes),
        scratch_shapes=list(scratch),
        name=name,
        compiler_params=pltpu.CompilerParams(vmem_limit_bytes=48 * 1024 * 1024),
    )(*args)
    return got[0] if single else got


def assemble(refs, scratch):
    mine = lax.axis_index("ch")
    for distance, ref in enumerate(refs):
        scratch[lax.bitwise_xor(mine, distance)] = ref[...]
    return (
        jnp.concatenate([scratch[0], scratch[1]], axis=1),
        jnp.concatenate([scratch[2], scratch[3]], axis=1),
    )


def project_kernel(geo, lengths, xo, xc, xy, xd, gain, w, normed, inputs, gates, near, far, scratch):
    tok = geo.tok
    width = w.shape[1]
    valid = geo.valid(lengths)
    sides = assemble((xo, xc, xy, xd), scratch)
    even = lax.rem(lax.axis_index("rows"), 2) == 0
    for half, side in enumerate(sides):
        first, last = side[:16], side[tok - 16 :]
        lanes = slice(half * width, (half + 1) * width)
        near[:, lanes] = jnp.where(even, last.astype(F32), first.astype(F32)).astype(BF16)
        far[:, lanes] = jnp.where(even, first.astype(F32), last.astype(F32)).astype(BF16)
    mover = permuter(tok)
    both = jnp.concatenate([w[0], w[1]], axis=1)
    for strand in range(2):
        side = sides[strand]
        if strand == 1:
            side = low(nn(side, mirror(width)))
        source = nn(mover, side)
        inverse = lax.rsqrt(jnp.mean(source * source, axis=-1, keepdims=True) + EPSILON)
        rows = low(source * inverse * gain[...])
        normed[strand] = rows
        out = nn(rows, both)
        lanes = out.shape[1] // 2
        inputs[strand] = low(out[:, :lanes] * valid)
        gates[strand] = out[:, lanes:]


def cotangent_kernel(geo, lengths, co, cc, cy, cd, gates, ow, moved, gm, dys, scratch):
    tok = geo.tok
    valid = geo.valid(lengths)
    sides = assemble((co, cc, cy, cd), scratch)
    mover = permuter(tok)
    for strand in range(2):
        side = sides[strand]
        if strand == 1:
            side = low(nn(side, mirror(side.shape[1])))
        rows = low(nn(mover, side))
        moved[strand] = rows
        grad = nt(rows, ow[...]) * valid
        gm[strand] = grad
        dys[strand] = grad * silu(gates[strand])


def rim_valid(geo, lengths_ref):
    _, offset, length = geo.place(lengths_ref)
    row = iota((32, 1), 0)
    token = jnp.where(row < 16, row - 16, geo.tok + row - 16) + offset
    index = token - offset + lax.axis_index("rows") * geo.tok
    inside = (token >= 0) & (token < geo.window) & (token < length)
    inside = inside & (index >= 0) & (index < geo.tok * geo.rows)
    return jnp.where(inside, 1.0, 0.0)


def fill_padded(padded, main, rims, steps):
    rim = padded.shape[0] // CHUNKS - steps
    rim = rim // 2
    lanes = main.shape[1]
    sub = iota((CHUNKS, lanes), 0)
    padded[rim * CHUNKS : (rim + steps) * CHUNKS] = main
    for k in range(1, rim + 1):
        block = main[(steps - k) * CHUNKS : (steps - k + 1) * CHUNKS]
        moved = pltpu.roll(block, 1, 0)
        edge = jnp.broadcast_to(rims[16 - k : 17 - k], (CHUNKS, lanes))
        padded[(rim - k) * CHUNKS : (rim - k + 1) * CHUNKS] = jnp.where(sub == 0, edge, moved)
    for k in range(rim):
        block = main[k * CHUNKS : (k + 1) * CHUNKS]
        moved = pltpu.roll(block, CHUNKS - 1, 0)
        edge = jnp.broadcast_to(rims[16 + k : 17 + k], (CHUNKS, lanes))
        at = rim + steps + k
        padded[at * CHUNKS : (at + 1) * CHUNKS] = jnp.where(sub == CHUNKS - 1, edge, moved)


def tap_start(tap, taps, flipped):
    return (2 * (taps - 1) - tap if flipped else tap) * CHUNKS


def conv_kernel(
    geo, lengths, inputs, near, far, gain, w, cw, cb, sw, padded, rims_normed, pre, act, message, select
):
    tok, steps = geo.tok, geo.steps
    taps = cw.shape[1]
    lanes = w.shape[2]
    width = w.shape[1]
    edge_valid = rim_valid(geo, lengths)
    even = lax.rem(lax.axis_index("rows"), 2) == 0
    select[...] = jnp.zeros_like(select)
    columns = sw.shape[2]
    for course in range(2):
        select[course, :, 64 * course : 64 * course + columns] = sw[course].astype(F32)
    for strand in range(2):
        part = slice(strand * width, (strand + 1) * width)
        one, two = near[:, part].astype(F32), far[:, part].astype(F32)
        source = jnp.concatenate([jnp.where(even, two, one), jnp.where(even, one, two)], axis=0)
        if strand == 1:
            source = nn(low(source), mirror(width))
        inverse = lax.rsqrt(jnp.mean(source * source, axis=-1, keepdims=True) + EPSILON)
        rows = low(source * inverse * gain[...])
        rims_normed[strand] = rows
        edges = low(nn(rows, w[0]) * edge_valid).astype(F32)
        main = inputs[strand].astype(F32)
        fill_padded(padded.at[strand], main, edges, steps)
        total = jnp.zeros((tok, LANES), F32)
        for course in range(2):
            member = 2 * strand + course
            running = jnp.broadcast_to(cb[course : course + 1], (tok, lanes))
            for tap in range(taps):
                at = tap_start(tap, taps, FLIPS[member])
                running = running + cw[course, tap : tap + 1] * padded[strand, at : at + tok]
            pre[member] = running
            active = low(silu(running))
            act[member] = active
            total = total + nn(active, low(select[course]))
        message[strand] = low(total)


def bcast(block, lane):
    return jnp.broadcast_to(block[:, lane : lane + 1], block.shape)


def summary_kernel(
    geo, lengths, one, two, act, dys, stw, stb, decay,
    proj, raw, step, drive, chunk_p, chunk_h, chunk_w, near, far, a2, up, down,
):
    tok, steps = geo.tok, geo.steps
    valid = geo.valid(lengths)
    for strand in range(2):
        total = one[strand].astype(F32) + two[strand].astype(F32)
        for course in range(2):
            member = 2 * strand + course
            here = total if course == 0 else pltpu.roll(total, 64, 1)
            proj[member] = here
            step_raw = nn(low(here)[:, :R], stw[course]) + stb[course : course + 1]
            step_row = softplus(step_raw) * valid
            raw[member] = step_raw
            step[member] = step_row
            drive[member] = step_row * act[member].astype(F32)
    for course in range(2):
        table = -LOG2E * jnp.exp(decay[course])
        for n in range(N):
            a2[course, n] = jnp.broadcast_to(table[n : n + 1], (CHUNKS, LANES))

    def sweep(member, flipped):
        strand, course = member // 2, lax.rem(member, 2)
        for base in range(0, N, 8):

            def body(k, carry):
                ps, hs, ws = carry
                t = steps - 1 - k if flipped else k
                rows = pl.ds(pl.multiple_of(t * CHUNKS, CHUNKS), CHUNKS)
                s, d, y = step[member, rows], drive[member, rows], dys[strand, rows]
                block = proj[member, rows]
                np_, nh, nw = [], [], []
                for i in range(8):
                    n = base + i
                    decay_here = jnp.exp2(s * a2[course, n])
                    p = ps[i] * decay_here
                    np_.append(p)
                    nh.append(hs[i] * decay_here + bcast(block, R + n) * d)
                    nw.append(ws[i] + p * (bcast(block, R + N + n) * y))
                return tuple(np_), tuple(nh), tuple(nw)

            zero = jnp.zeros((CHUNKS, LANES), F32)
            start = (tuple([zero + 1.0] * 8), (zero,) * 8, (zero,) * 8)
            ps, hs, ws = lax.fori_loop(0, steps, body, start, unroll=2)
            for i in range(8):
                rows = slice((base + i) * CHUNKS, (base + i + 1) * CHUNKS)
                chunk_p[member, rows] = ps[i]
                chunk_h[member, rows] = hs[i]
                chunk_w[member, rows] = ws[i]

    lax.fori_loop(0, 2, lambda i, c: (sweep(3 * i, False), c)[1], 0)
    lax.fori_loop(0, 2, lambda i, c: (sweep(1 + i, True), c)[1], 0)

    slots = {0: (0, 2), 3: (1, 3), 1: (2, 0), 2: (3, 1)}
    for member in range(4):
        h = jnp.zeros((N, LANES), F32)
        w = jnp.zeros((N, LANES), F32)
        order = list(range(CHUNKS))
        forward = order[::-1] if FLIPS[member] else order
        for j in forward:
            rows = pl.ds(j, N, stride=CHUNKS)
            h = chunk_p[member, rows] * h + chunk_h[member, rows]
        for j in forward[::-1]:
            rows = pl.ds(j, N, stride=CHUNKS)
            w = chunk_p[member, rows] * w + chunk_w[member, rows]
        length = jnp.sum(step[member], axis=0, keepdims=True)
        slot_up, slot_down = slots[member]
        goes_up, goes_down = (w, h) if FLIPS[member] else (h, w)
        up[slot_up * N : (slot_up + 1) * N] = goes_up
        down[slot_down * N : (slot_down + 1) * N] = goes_down
        up[4 * N + slot_up : 4 * N + slot_up + 1] = length
        down[4 * N + slot_down : 4 * N + slot_down + 1] = length
    up[4 * N + 4 :] = jnp.zeros((4, LANES), F32)
    down[4 * N + 4 :] = jnp.zeros((4, LANES), F32)
    if near is not None:
        local = geo.local()
        near[...] = jnp.where(lax.rem(local, 2) == 0, up[...], down[...])
        far[...] = jnp.where(local < 2, up[...], down[...])


UP_MEMBERS = (0, 3, 1, 2)
DOWN_MEMBERS = (1, 2, 0, 3)


def scan_kernel(
    geo, lengths, slot_refs, act, proj, raw, step, drive, chunk_p, chunk_h, chunk_w,
    dys, gm, gates, stw, decay, skip,
    mixed, dgate, dact, message, small,
    slots, a2, a1, enter, adjoint, states, quads, picks, out_y, slope_y, pull_y, dproj, dacc,
):
    tok, steps = geo.tok, geo.steps
    count = geo.members
    valid = geo.valid(lengths)
    row = lax.axis_index("rows")
    local = geo.local()
    base_row = row - local
    if len(slot_refs) == 1:
        slots = slot_refs[0]
    else:
        slots[local] = jnp.zeros(slots.shape[1:], F32)
        others = (lax.bitwise_xor(local, 1), lax.rem(local + 2, 4), 3 - local)
        for at, ref in zip(others, slot_refs):
            slots[at] = ref[...]
    for course in range(2):
        natural = -jnp.exp(decay[course])
        for n in range(N):
            wide = jnp.broadcast_to(natural[n : n + 1], (CHUNKS, LANES))
            a1[course, n] = wide
            a2[course, n] = wide * LOG2E
    depth = picks.shape[0]
    picks[...] = one_hot(iota((depth, LANES), 1) == R + iota((depth, LANES), 0) // LANES)
    dacc[...] = jnp.zeros_like(dacc)

    def fold(ascending, carried):
        members = UP_MEMBERS if ascending else DOWN_MEMBERS
        tables = [-LOG2E * jnp.exp(decay[m % 2]) for m in members]

        def one(i, carried):
            k = i if ascending else count - 1 - i
            there = base_row + k
            use = (k < local) if ascending else (k > local)
            use = use & (there >= 0) & (there < geo.rows)
            out = []
            for q in range(4):
                length = slots[k, 4 * N + q : 4 * N + q + 1]
                new = jnp.exp2(tables[q] * length) * carried[q] + slots[k, q * N : (q + 1) * N]
                out.append(jnp.where(use, new, carried[q]))
            return tuple(out)

        return lax.fori_loop(0, count, one, carried)

    zero = (jnp.zeros((N, LANES), F32),) * 4
    from_below = fold(True, zero)
    from_above = fold(False, zero)
    order = list(range(CHUNKS))
    for q in range(4):
        for value, member, js in (
            (from_below[q], UP_MEMBERS[q], order),
            (from_above[q], DOWN_MEMBERS[q], order[::-1]),
        ):
            target, source = (enter, chunk_h) if q < 2 else (adjoint, chunk_w)
            for j in js:
                rows = pl.ds(j, N, stride=CHUNKS)
                target[member, rows] = value
                value = chunk_p[member, rows] * value + source[member, rows]

    def sweep(member, flipped):
        strand, course = member // 2, lax.rem(member, 2)
        states[: N * CHUNKS] = enter[member]

        def ahead(i, carry):
            hs = list(carry)
            kept = []
            for sub in range(2):
                k = 2 * i + sub
                t = steps - 1 - k if flipped else k
                rows = pl.ds(pl.multiple_of(t * CHUNKS, CHUNKS), CHUNKS)
                s, d, y = step[member, rows], drive[member, rows], dys[strand, rows]
                block = proj[member, rows]
                total = jnp.zeros((CHUNKS, LANES), F32)
                products = []
                for n in range(N):
                    hs[n] = hs[n] * jnp.exp2(s * a2[course, n]) + bcast(block, R + n) * d
                    total = total + bcast(block, R + N + n) * hs[n]
                    products.append(y * hs[n])
                    at = pl.multiple_of(((k + 1) * N + n) * CHUNKS, CHUNKS)
                    states[pl.ds(at, CHUNKS)] = hs[n]
                out_y[member, rows] = total
                kept.append(products)
            pair = steps // 2 - 1 - i if flipped else i
            rows = pl.ds(pl.multiple_of(pair * 16, 16), 16)
            first, second = (kept[1], kept[0]) if flipped else (kept[0], kept[1])
            for n in range(N):
                both = low(jnp.concatenate([first[n], second[n]], axis=0))
                quads[rows, (N + n) * LANES : (N + n + 1) * LANES] = both
            return tuple(hs)

        start = tuple(enter[member, n * CHUNKS : (n + 1) * CHUNKS] for n in range(N))
        lax.fori_loop(0, steps // 2, ahead, start)

        def back(i, carry):
            cs, ds = list(carry[0]), list(carry[1])
            kept = []
            for sub in range(2):
                k = steps - 1 - (2 * i + sub)
                t = steps - 1 - k if flipped else k
                rows = pl.ds(pl.multiple_of(t * CHUNKS, CHUNKS), CHUNKS)
                s, d, y = step[member, rows], drive[member, rows], dys[strand, rows]
                block = proj[member, rows]
                pulled = jnp.zeros((CHUNKS, LANES), F32)
                slope = jnp.zeros((CHUNKS, LANES), F32)
                products = []
                for n in range(N):
                    lam = y * bcast(block, R + N + n) + cs[n]
                    pulled = pulled + lam * bcast(block, R + n)
                    products.append(lam * d)
                    cs[n] = lam * jnp.exp2(s * a2[course, n])
                    at = pl.multiple_of((k * N + n) * CHUNKS, CHUNKS)
                    u = cs[n] * states[pl.ds(at, CHUNKS)]
                    slope = slope + u * a1[course, n]
                    ds[n] = ds[n] + u * s
                slope_y[member, rows] = slope
                pull_y[member, rows] = pulled
                kept.append(products)
            pair = i if flipped else steps // 2 - 1 - i
            rows = pl.ds(pl.multiple_of(pair * 16, 16), 16)
            first, second = (kept[0], kept[1]) if flipped else (kept[1], kept[0])
            for n in range(N):
                both = low(jnp.concatenate([first[n], second[n]], axis=0))
                quads[rows, n * LANES : (n + 1) * LANES] = both
            return tuple(cs), tuple(ds)

        start = tuple(adjoint[member, n * CHUNKS : (n + 1) * CHUNKS] for n in range(N))
        zeros = (jnp.zeros((CHUNKS, LANES), F32),) * N
        _, ds = lax.fori_loop(0, steps // 2, back, (start, zeros))
        for n in range(N):
            rows = slice(n * CHUNKS, (n + 1) * CHUNKS)
            dacc[course, rows] = dacc[course, rows] + ds[n]
        dproj[member] = nn(quads[...], picks[...])

    lax.fori_loop(0, 2, lambda i, c: (sweep(3 * i, False), c)[1], 0)
    lax.fori_loop(0, 2, lambda i, c: (sweep(1 + i, True), c)[1], 0)

    small[...] = jnp.zeros_like(small)
    for course in range(2):
        for n in range(N):
            total = jnp.sum(dacc[course, n * CHUNKS : (n + 1) * CHUNKS], axis=0, keepdims=True)
            at = 2 * R + course * N + n
            small[at : at + 1] = total * a1[course, n, :1]
    for strand in range(2):
        joined = jnp.zeros((tok, LANES), F32)
        sent = jnp.zeros((tok, LANES), F32)
        grad = dys[strand]
        for course in range(2):
            member = 2 * strand + course
            active = act[member].astype(F32)
            joined = joined + out_y[member] + skip[course : course + 1] * active
            raw_grad = slope_y[member] + pull_y[member] * active
            rounded = low(raw_grad * valid * sigmoid(raw[member]))
            dact[member] = pull_y[member] * step[member] + grad * skip[course : course + 1]
            rows = slice(course * R, (course + 1) * R)
            small[rows] += tn(low(proj[member]), rounded)[:R]
            at = 2 * R + 2 * N + course
            small[at : at + 1] += jnp.sum(rounded.astype(F32), axis=0, keepdims=True)
            small[at + 2 : at + 3] += jnp.sum(grad * active, axis=0, keepdims=True)
            wide = jnp.concatenate([stw[course], jnp.zeros((LANES - R, LANES), BF16)], axis=0)
            here = dproj[member] + nt(rounded, wide)
            sent = sent + (here if course == 0 else pltpu.roll(here, 64, 1))
        message[strand] = low(sent)
        gate = gates[strand]
        mixed[strand] = low(joined * silu(gate) * valid)
        dgate[strand] = low(gm[strand] * joined * silu_slope(gate))


def dense_kernel(geo, mixed, ow, moved, dgate, normed, w, kept, sent, g_out, g_gate, dn_gate):
    tok = geo.tok
    mover = unpermuter(tok)
    width = w.shape[1]
    turn = mirror(width)
    second = lax.axis_index("ch") >= 2
    branches = []
    grad_out = jnp.zeros(g_out.shape, F32)
    grad_gate = jnp.zeros(g_gate.shape, F32)
    for strand in range(2):
        out_w, gate_w = ow[...], w[1]
        if strand == 1:
            out_w, gate_w = low(nn(out_w, turn)), low(nn(turn, gate_w))
        branches.append(nn(low(nn(mover, mixed[strand])), out_w))
        grad_out = grad_out + tn(mixed[strand], moved[strand])
        grad_gate = grad_gate + tn(normed[strand], dgate[strand])
        dn_gate[strand] = nt(low(nn(mover, dgate[strand])), gate_w)
    kept[...] = jnp.where(second, branches[1], branches[0])
    sent[...] = low(jnp.where(second, branches[0], branches[1]))
    g_out[...] = grad_out
    g_gate[...] = grad_gate


GRAD_ROWS = 992


def conv_back_kernel(
    geo, lengths, one, two, act, dact, pre, padded, cw, select, normed, rims_normed, gain, w,
    g_gate, g_out, small, res_kept, res_got,
    xg, near, far, keep, send, gain_part, res_own, res_sent,
    pad_grad, pack,
):
    tok, steps = geo.tok, geo.steps
    taps = cw.shape[1]
    width = w.shape[1]
    valid = geo.valid(lengths)
    edge_valid = rim_valid(geo, lengths)
    even = lax.rem(lax.axis_index("rows"), 2) == 0
    rim = taps - 1
    sub = iota((CHUNKS, LANES), 0)
    pack[...] = jnp.zeros_like(pack)
    grad_select = jnp.zeros((LANES, LANES), F32)
    grad_in = jnp.zeros((width, LANES), F32)
    at_conv = 3 * width + LANES
    for strand in range(2):
        pad_grad[...] = jnp.zeros_like(pad_grad)
        rounded = low(one[strand].astype(F32) + two[strand].astype(F32))
        lane = iota((LANES, LANES), 1)
        for course in range(2):
            member = 2 * strand + course
            here = tn(act[member], rounded)
            grad_select = grad_select + jnp.where((lane >= 64) == (course == 1), here, 0.0)
            total = dact[member] + nt(rounded, low(select[course]))
            grad = total * silu_slope(pre[member])
            row = at_conv + 8 + course
            pack[row : row + 1] += jnp.sum(grad, axis=0, keepdims=True)
            for tap in range(taps):
                at = tap_start(tap, taps, FLIPS[member])
                row = at_conv + course * taps + tap
                pack[row : row + 1] += jnp.sum(grad * padded[strand, at : at + tok], axis=0, keepdims=True)
                pad_grad[at : at + tok] += cw[course, tap : tap + 1] * grad
        before = [jnp.zeros((1, LANES), F32)] * (16 - rim)
        after = []
        for k in range(rim, 0, -1):
            block = pad_grad[(rim - k) * CHUNKS : (rim - k + 1) * CHUNKS]
            before.append(block[:1])
            moved = jnp.where(sub == CHUNKS - 1, 0.0, pltpu.roll(block, CHUNKS - 1, 0))
            at = (rim + steps - k) * CHUNKS
            pad_grad[at : at + CHUNKS] += moved
        for k in range(rim):
            at = (rim + steps + k) * CHUNKS
            block = pad_grad[at : at + CHUNKS]
            after.append(block[CHUNKS - 1 :])
            moved = jnp.where(sub == 0, 0.0, pltpu.roll(block, 1, 0))
            at = (rim + k) * CHUNKS
            pad_grad[at : at + CHUNKS] += moved
        after += [jnp.zeros((1, LANES), F32)] * (16 - rim)
        rims = jnp.concatenate(before + after, axis=0) * edge_valid
        main = pad_grad[rim * CHUNKS : (rim + steps) * CHUNKS]
        xg[strand] = main
        grad_in = grad_in + tn(normed[strand], low(main * valid)) + tn(rims_normed[strand], low(rims))
        near[strand] = jnp.where(even, rims[16:], rims[:16])
        far[strand] = jnp.where(even, rims[:16], rims[16:])
    pack[:width] = grad_in
    pack[width : 2 * width] = g_gate[...]
    pack[2 * width : 2 * width + LANES] = g_out[:, :LANES]
    pack[2 * width + LANES : 3 * width] = g_out[:, LANES:]
    pack[3 * width : at_conv] = grad_select
    pack[at_conv + 16 : at_conv + 16 + small.shape[0]] = small[...]
    product = grad_in * w[0].astype(F32) + g_gate[...] * w[1].astype(F32)
    high = low(product)
    ones = jnp.ones((8, LANES), BF16)
    gain_part[...] = (nt(ones, high) + nt(ones, low(product - high.astype(F32)))) / gain[...]
    half = GRAD_ROWS // 2
    if keep.shape[0] == GRAD_ROWS:
        keep[...] = pack[...]
    else:
        mine = lax.rem(lax.axis_index("rows"), 2)
        keep[...] = pack[pl.ds(pl.multiple_of(mine * half, 16), half)]
        send[...] = low(pack[pl.ds(pl.multiple_of((1 - mine) * half, 16), half)])
    total = res_kept[...] + res_got[...].astype(F32)
    odd = lax.rem(lax.axis_index("ch"), 2) == 1
    res_own[...] = jnp.where(odd, total[:, LANES:], total[:, :LANES])
    res_sent[...] = low(jnp.where(odd, total[:, :LANES], total[:, LANES:]))


def normed_back_kernel(geo, lengths, xg, near, far, dn_gate, w, hidden, res_own, res_got, kept, sent, result):
    tok, steps = geo.tok, geo.steps
    valid = geo.valid(lengths)
    even = lax.rem(lax.axis_index("rows"), 2) == 0
    mover = unpermuter(tok)
    turn = mirror(w.shape[1])
    second = lax.axis_index("ch") >= 2
    row = iota((tok, LANES), 0)
    token = (row % CHUNKS) * steps + row // CHUNKS
    grads = []
    for strand in range(2):
        one, two = near[strand], far[strand]
        ahead = jnp.where(even, two, one)
        behind = jnp.where(even, one, two)
        total = xg[strand]
        for k in range(3):
            total = total + jnp.where(token == k, ahead[k : k + 1], 0.0)
            total = total + jnp.where(token == tok - 1 - k, behind[15 - k : 16 - k], 0.0)
        rounded = low(total * valid)
        in_w = w[0]
        if strand == 1:
            in_w = low(nn(turn, in_w))
        grads.append(nt(low(nn(mover, rounded)), in_w) + dn_gate[strand])
    kept[...] = jnp.where(second, grads[1], grads[0])
    sent[...] = low(jnp.where(second, grads[0], grads[1]))
    out = hidden[...].astype(F32) + res_own[...] + res_got[...].astype(F32)
    result[...] = low(out)


def finish_kernel(geo, one, two, xo, xc, gain, cot, input_grad):
    width = one.shape[1]
    mine = lax.axis_index("ch")
    odd = lax.rem(mine, 2) == 1
    a, b = xo[...].astype(F32), xc[...].astype(F32)
    source = jnp.concatenate([jnp.where(odd, b, a), jnp.where(odd, a, b)], axis=1)
    inverse = lax.rsqrt(jnp.mean(source * source, axis=-1, keepdims=True) + EPSILON)
    unit = source * inverse
    plain = jnp.broadcast_to(gain[...], (8, width))
    high = low(plain)
    rest = plain - high.astype(F32)
    middle = low(rest)
    turn = mirror(width)
    turned = nn(high, turn) + nn(middle, turn) + nn(low(rest - middle.astype(F32)), turn)
    here = jnp.where(mine >= 2, turned, plain)[:1]
    scaled = (one[...].astype(F32) + two[...].astype(F32)) * here
    back = inverse * (scaled - unit * jnp.mean(scaled * unit, axis=-1, keepdims=True))
    input_grad[...] = cot[...].astype(F32) + jnp.where(odd, back[:, LANES:], back[:, :LANES])


def unpack_kernel(halves, gain_sum, in_g, out_g, sel_g, cw_g, cb_g, stw_g, stb_g, decay_g, skip_g, gain_g, pack):
    if len(halves) == 1:
        pack[...] = halves[0][...].astype(F32)
    else:
        half = GRAD_ROWS // 2
        mine = lax.rem(lax.axis_index("rows"), 2)
        pack[pl.ds(pl.multiple_of(mine * half, 16), half)] = halves[0][...].astype(F32)
        pack[pl.ds(pl.multiple_of((1 - mine) * half, 16), half)] = halves[1][...].astype(F32)
    width = in_g.shape[1]
    in_g[0] = pack[:width]
    in_g[1] = pack[width : 2 * width]
    out_g[:, :LANES] = pack[2 * width : 2 * width + LANES]
    out_g[:, LANES:] = pack[2 * width + LANES : 3 * width]
    at = 3 * width + LANES
    select = pack[3 * width : at]
    columns = sel_g.shape[2]
    sel_g[0] = select[:, :columns]
    sel_g[1] = pltpu.roll(select, 64, 1)[:, :columns]
    taps = cw_g.shape[1]
    for course in range(2):
        cw_g[course] = pack[at + course * taps : at + (course + 1) * taps]
    cb_g[...] = pack[at + 2 * taps : at + 2 * taps + 2]
    at = at + 16
    for course in range(2):
        stw_g[course] = pack[at + course * R : at + (course + 1) * R]
        decay_g[course] = pack[at + 2 * R + course * N : at + 2 * R + (course + 1) * N]
    at = at + 2 * R + 2 * N
    stb_g[...] = pack[at : at + 2]
    skip_g[...] = pack[at + 2 : at + 4]
    gain_g[...] = gain_sum[:1]


def swap(value, axis, distance):
    count = lax.axis_size(axis)
    return lax.ppermute(value, axis, [(i, i ^ distance) for i in range(count)])


def gather_channels(value):
    across = swap(value, "ch", 2)
    return value, swap(value, "ch", 1), across, swap(across, "ch", 1)


def partner_sum(value):
    joined = low(value.astype(F32) + swap(value, "ch", 2).astype(F32))
    return joined, swap(joined, "ch", 1)


def on_device(
    hidden_in, lengths, norm_gain, in_weight, conv_weight, conv_bias, select_weight,
    step_weight, step_bias, decay_log, skip_gain, out_weight, cotangent,
):
    tok = hidden_in.shape[0]
    rows = lax.axis_size("rows")
    geo = Geometry(tok, rows)
    steps = geo.steps
    width = in_weight.shape[1]
    gain = norm_gain[None, :]
    small_mesh = geo.members == 4 and rows == 8
    padded_rows = (steps + 2 * (conv_weight.shape[1] - 1)) * CHUNKS

    def kernel(f):
        return functools.partial(f, geo)

    def lifted(f, first, amount):
        def body(*refs):
            return f(*refs[:first], refs[first : first + amount], *refs[first + amount :])

        return body

    x_parts = gather_channels(hidden_in)
    c_parts = gather_channels(cotangent)

    normed, inputs, gates, near, far = run(
        kernel(project_kernel),
        [
            ((2, tok, width), BF16),
            ((2, tok, LANES), BF16),
            ((2, tok, LANES), F32),
            ((16, 2 * width), BF16),
            ((16, 2 * width), BF16),
        ],
        lengths, *x_parts, gain, in_weight,
        smem=1, scratch=[pltpu.VMEM((4, tok, LANES), BF16)], name="project",
    )
    near = lax.ppermute(near, "rows", geo.near())
    far = lax.ppermute(far, "rows", geo.far())
    moved, gm, dys = run(
        kernel(cotangent_kernel),
        [((2, tok, width), BF16), ((2, tok, LANES), F32), ((2, tok, LANES), F32)],
        lengths, *c_parts, gates, out_weight,
        smem=1, scratch=[pltpu.VMEM((4, tok, LANES), BF16)], name="cotangents",
    )
    padded, rims_normed, pre, act, message, select = run(
        kernel(conv_kernel),
        [
            ((2, padded_rows, LANES), F32),
            ((2, 32, width), BF16),
            ((4, tok, LANES), F32),
            ((4, tok, LANES), BF16),
            ((2, tok, LANES), BF16),
            ((2, LANES, LANES), F32),
        ],
        lengths, inputs, near, far, gain, in_weight, conv_weight, conv_bias, select_weight,
        smem=1, name="conv",
    )
    one, two = partner_sum(message)
    chunked = ((4, N * CHUNKS, LANES), F32)
    summary = ((4 * N + 8, LANES), F32)
    members = ((4, tok, LANES), F32)
    outs = [members, members, members, members, chunked, chunked, chunked]
    table = pltpu.VMEM((2, N, CHUNKS, LANES), F32)
    if small_mesh:

        def summarise(*refs):
            ins, out, rest = refs[:8], refs[8:15], refs[15:]
            near_ref, far_ref, a2, up, down = rest
            summary_kernel(geo, *ins, *out, near_ref, far_ref, a2, up, down)

        scratch = [table, pltpu.VMEM(summary[0], F32), pltpu.VMEM(summary[0], F32)]
    else:

        def summarise(*refs):
            ins, out, rest = refs[:8], refs[8:15], refs[15:]
            up, down, a2 = rest
            summary_kernel(geo, *ins, *out, None, None, a2, up, down)

        scratch = [table]
    got = run(
        summarise, outs + [summary, summary],
        lengths, one, two, act, dys, step_weight, step_bias, decay_log,
        smem=1, scratch=scratch, name="summary",
    )
    proj, raw, step, drive, chunk_p, chunk_h, chunk_w = got[:7]
    if small_mesh:
        slots = (
            lax.ppermute(got[7], "rows", geo.near()),
            lax.ppermute(got[8], "rows", geo.across()),
            lax.ppermute(got[8], "rows", geo.far()),
        )
        slot_scratch = pltpu.VMEM((4,) + summary[0], F32)
    else:
        up, down = lax.all_gather(got[7], "rows"), lax.all_gather(got[8], "rows")
        place = lax.axis_index("rows")
        base = place - geo.local()
        index = base + jnp.arange(geo.members)
        inside = jnp.clip(index, 0, rows - 1)
        slots = (jnp.where((index < place)[:, None, None], up[inside], down[inside]),)
        slot_scratch = pltpu.VMEM((8, LANES), F32)
    mixed, dgate, dact, message, small = run(
        lifted(kernel(scan_kernel), 1, len(slots)),
        [
            ((2, tok, LANES), BF16),
            ((2, tok, LANES), BF16),
            members,
            ((2, tok, LANES), BF16),
            ((80, LANES), F32),
        ],
        lengths, *slots, act, proj, raw, step, drive, chunk_p, chunk_h, chunk_w,
        dys, gm, gates, step_weight, decay_log, skip_gain,
        smem=1,
        scratch=[
            slot_scratch,
            table,
            table,
            pltpu.VMEM(chunked[0], F32),
            pltpu.VMEM(chunked[0], F32),
            pltpu.VMEM(((steps + 1) * N * CHUNKS, LANES), F32),
            pltpu.VMEM((tok, 2 * N * LANES), BF16),
            pltpu.VMEM((2 * N * LANES, LANES), BF16),
            pltpu.VMEM(members[0], F32),
            pltpu.VMEM(members[0], F32),
            pltpu.VMEM(members[0], F32),
            pltpu.VMEM(members[0], F32),
            pltpu.VMEM((2, N * CHUNKS, LANES), F32),
        ],
        name="scan",
    )
    one, two = partner_sum(message)
    res_kept, res_sent, g_out, g_gate, dn_gate = run(
        kernel(dense_kernel),
        [
            ((tok, width), F32),
            ((tok, width), BF16),
            ((LANES, width), F32),
            ((width, LANES), F32),
            ((2, tok, width), F32),
        ],
        mixed, out_weight, moved, dgate, normed, in_weight, name="dense",
    )
    res_got = swap(res_sent, "ch", 2)
    half = GRAD_ROWS // 2
    xg, near, far, keep, send, gain_part, res_own, res_sent = run(
        kernel(conv_back_kernel),
        [
            ((2, tok, LANES), F32),
            ((2, 16, LANES), F32),
            ((2, 16, LANES), F32),
            ((half if small_mesh else GRAD_ROWS, LANES), F32),
            ((half, LANES), BF16),
            ((8, width), F32),
            ((tok, LANES), F32),
            ((tok, LANES), BF16),
        ],
        lengths, one, two, act, dact, pre, padded, conv_weight, select, normed, rims_normed, gain, in_weight,
        g_gate, g_out, small, res_kept, res_got,
        smem=1, scratch=[pltpu.VMEM((padded_rows, LANES), F32), pltpu.VMEM((GRAD_ROWS, LANES), F32)],
        name="conv_back",
    )
    if small_mesh:
        grads = low(keep + swap(send, "rows", 1).astype(F32))
        others = [swap(grads, "rows", d) for d in (2, 4, 6)]
    near = lax.ppermute(near, "rows", geo.near())
    far = lax.ppermute(far, "rows", geo.far())
    res_got = swap(res_sent, "ch", 1)
    dn_kept, dn_sent, result = run(
        kernel(normed_back_kernel),
        [((tok, width), F32), ((tok, width), BF16), ((tok, LANES), BF16)],
        lengths, xg, near, far, dn_gate, in_weight, hidden_in, res_own, res_got,
        smem=1, name="normed_back",
    )
    dn = low(dn_kept + swap(dn_sent, "ch", 2).astype(F32))
    input_grad = run(
        kernel(finish_kernel), ((tok, LANES), F32),
        dn, swap(dn, "ch", 1), x_parts[0], x_parts[1], gain, cotangent, name="finish",
    )
    if small_mesh:
        gain_part = gain_part + swap(gain_part, "ch", 2)
        gain_part = gain_part + swap(gain_part, "ch", 1)
        gain_part = gain_part + swap(gain_part, "rows", 1)
        gain_part = gain_part + sum(swap(gain_part, "rows", d) for d in (2, 4, 6))
        grads = low(sum((g.astype(F32) for g in others), grads.astype(F32)))
        halves = (grads, swap(grads, "rows", 1))
    else:
        gain_part = lax.psum(gain_part, ("rows", "ch"))
        halves = (lax.psum(keep, "rows"),)
    got = run(
        lifted(unpack_kernel, 0, len(halves)),
        [
            (in_weight.shape, F32),
            (out_weight.shape, F32),
            (select_weight.shape, F32),
            (conv_weight.shape, F32),
            (conv_bias.shape, F32),
            (step_weight.shape, F32),
            (step_bias.shape, F32),
            (decay_log.shape, F32),
            (skip_gain.shape, F32),
            ((1, width), F32),
        ],
        *halves, gain_part, scratch=[pltpu.VMEM((GRAD_ROWS, LANES), F32)], name="unpack",
    )
    in_g, out_g, sel_g, cw_g, cb_g, stw_g, stb_g, decay_g, skip_g, gain_g = got
    return (
        result, input_grad, gain_g[0], in_g, cw_g, cb_g, sel_g, stw_g, stb_g, decay_g, skip_g, out_g,
    )


def solution(mesh):
    lanes = P(None, None, "ch")
    pair = P(None, "ch")
    columns = P(None, "ch", None)
    tokens = P("rows", "ch")
    return jax.shard_map(
        on_device,
        mesh=mesh,
        in_specs=(
            tokens, P(), P(), lanes, lanes, pair, columns, lanes, pair, lanes, pair, P("ch", None), tokens,
        ),
        out_specs=(
            tokens, tokens, P(), lanes, lanes, pair, columns, lanes, pair, lanes, pair, P("ch", None),
        ),
        check_vma=False,
    )
```

```python
import functools

import jax
import jax.numpy as jnp
from jax import lax
from jax.experimental import pallas as pl
from jax.experimental.pallas import tpu as pltpu
from jax.sharding import PartitionSpec as P

N = 16
R = 16
WINDOW = 16384
LANES = 128
CHUNKS = 8
EPSILON = 1e-06
LOG2E = 1.4426950408889634
F32 = jnp.float32
BF16 = jnp.bfloat16
VM = pl.BlockSpec(memory_space=pltpu.VMEM)
FLIPS = (False, True, True, False)


def nn(left, right):
    return lax.dot_general(left, right, (((1,), (0,)), ((), ())), preferred_element_type=F32)


def nt(left, right):
    return lax.dot_general(left, right, (((1,), (1,)), ((), ())), preferred_element_type=F32)


def tn(left, right):
    return lax.dot_general(left, right, (((0,), (0,)), ((), ())), preferred_element_type=F32)


def iota(shape, dim):
    return lax.broadcasted_iota(jnp.int32, shape, dim)


def one_hot(mask):
    return jnp.where(mask, 1.0, 0.0).astype(BF16)


def permuter(tok):
    steps = tok // CHUNKS
    row, col = iota((tok, tok), 0), iota((tok, tok), 1)
    return one_hot((row % CHUNKS) * steps + row // CHUNKS == col)


def unpermuter(tok):
    steps = tok // CHUNKS
    row, col = iota((tok, tok), 0), iota((tok, tok), 1)
    return one_hot((col % CHUNKS) * steps + col // CHUNKS == row)


def mirror(width):
    return one_hot(iota((width, width), 0) + iota((width, width), 1) == width - 1)


def sigmoid(v):
    return 1.0 / (1.0 + jnp.exp(-v))


def silu(v):
    return v * sigmoid(v)


def silu_slope(v):
    logistic = sigmoid(v)
    return logistic * (1.0 + v * (1.0 - logistic))


def softplus(v):
    return jnp.maximum(v, 0.0) + jnp.log1p(jnp.exp(-jnp.abs(v)))


def low(v):
    return v.astype(BF16)


class Geometry:
    def __init__(self, tok, rows):
        self.tok = tok
        self.rows = rows
        self.window = min(WINDOW, tok * rows // 2)
        self.members = self.window // tok
        self.steps = tok // CHUNKS

    def place(self, lengths_ref):
        row = lax.axis_index("rows")
        shifted = row * self.tok + self.window // 2
        offset = lax.rem(shifted, self.window)
        length = lengths_ref[lax.div(shifted, self.window)]
        return row, offset, length

    def valid(self, lengths_ref):
        _, offset, length = self.place(lengths_ref)
        row = iota((self.tok, 1), 0)
        token = (row % CHUNKS) * self.steps + row // CHUNKS
        return jnp.where(offset + token < length, 1.0, 0.0)

    def local(self):
        row = lax.axis_index("rows")
        return lax.rem(row + self.members // 2, self.members)

    def near(self):
        return [(i, i ^ 1) for i in range(self.rows)]

    def far(self):
        if self.members == 4:
            return self.swaps(lambda k: 3 - k)
        out = []
        for i in range(1, self.rows, 2):
            out += [(i, (i + 1) % self.rows), ((i + 1) % self.rows, i)]
        return out

    def across(self):
        return self.swaps(lambda k: (k + 2) % 4)

    def swaps(self, other):
        out = []
        for i in range(self.rows):
            local = (i + 2) % 4
            j = i - local + other(local)
            out.append((i, j if 0 <= j < self.rows else i ^ 1))
        return out


def run(kernel, outs, *args, anywhere=0, scratch=(), name=None, micros=1):
    single = isinstance(outs, tuple)
    shapes = [outs] if single else list(outs)
    args = [pltpu.with_memory_space_constraint(a, pltpu.HBM) for a in args[:anywhere]] + list(args[anywhere:])
    got = pl.pallas_call(
        kernel,
        out_shape=[jax.ShapeDtypeStruct(s, d) for s, d in shapes],
        in_specs=[pl.BlockSpec(memory_space=pltpu.HBM)] * anywhere + [VM] * (len(args) - anywhere),
        out_specs=[VM] * len(shapes),
        scratch_shapes=list(scratch),
        name=name,
        compiler_params=pltpu.CompilerParams(vmem_limit_bytes=48 * 1024 * 1024),
        cost_estimate=pl.CostEstimate(flops=0, bytes_accessed=int(micros * 3.0e6), transcendentals=0),
    )(*args)
    return got[0] if single else got


def assemble(refs, scratch):
    mine = lax.axis_index("ch")
    for distance, ref in enumerate(refs):
        scratch[lax.bitwise_xor(mine, distance)] = ref[...]
    return (
        jnp.concatenate([scratch[0], scratch[1]], axis=1),
        jnp.concatenate([scratch[2], scratch[3]], axis=1),
    )


def prepare_kernel(
    geo, lengths_in, x_in, c_in, w_in, ow_in, stw_in, gain_in, cw_in, cb_in, sw_in, stb_in, decay_in, skip_in,
    x_out, c_out, valid, edge, turn, mover, back, gains, weights, outs, select, table, spread, tiny, stw,
    lengths, gain, cw, cb, sw, stb, decay, skip, sems,
):
    pairs = (
        (lengths_in, lengths), (w_in, weights.at[0:2]), (ow_in, outs.at[0]), (stw_in, stw), (gain_in, gain),
        (cw_in, cw), (cb_in, cb), (sw_in, sw), (stb_in, stb), (decay_in, decay), (skip_in, skip),
        (x_in, x_out), (c_in, c_out),
    )
    copies = [pltpu.make_async_copy(source, target, sems.at[i]) for i, (source, target) in enumerate(pairs)]
    for copy in copies:
        copy.start()
    tok = geo.tok
    width = turn.shape[0]
    flip = mirror(width)
    turn[...] = flip
    mover[...] = permuter(tok)
    back[...] = unpermuter(tok)
    for at in range(0, 2 * N):
        key = iota((LANES, LANES), 0) % 64
        spread[:, at * LANES : (at + 1) * LANES] = one_hot(key == R + at)
    select[...] = jnp.zeros_like(select)
    tiny[...] = jnp.zeros_like(tiny)
    for copy in copies:
        copy.wait()
    valid[...] = jnp.broadcast_to(geo.valid(lengths), valid.shape)
    edge[...] = jnp.broadcast_to(rim_valid(geo, lengths), edge.shape)
    plain = jnp.broadcast_to(gain[...], (8, width))
    high = low(plain)
    rest = plain - high.astype(F32)
    middle = low(rest)
    turned = nn(high, flip) + nn(middle, flip) + nn(low(rest - middle.astype(F32)), flip)
    gains[:1] = gain[...]
    gains[1:] = turned[:1]
    for k in range(2):
        weights[2 + k] = low(nn(flip, weights[k]))
    outs[1] = low(nn(outs[0], flip))
    amount = sw.shape[1]
    for course in range(2):
        select[course, 64 * course : 64 * course + amount] = sw[course]
        natural = -jnp.exp(decay[course])
        for n in range(N):
            level = jnp.broadcast_to(natural[n : n + 1], (CHUNKS, LANES))
            table[course, n] = level
            table[2 + course, n] = level * LOG2E
    taps = cw.shape[1]
    for course in range(2):
        tiny[course * taps : (course + 1) * taps] = cw[course]
        tiny[24 + course * N : 24 + (course + 1) * N] = -LOG2E * jnp.exp(decay[course])
    tiny[8:10] = cb[...]
    tiny[10:12] = stb[...]
    tiny[12:14] = skip[...]


def project_kernel(geo, xo, xc, xy, xd, valid, turn, mover, gains, w, normed, inputs, gates, near, far, scratch):
    tok = geo.tok
    width = w.shape[1]
    sides = assemble((xo, xc, xy, xd), scratch)
    even = lax.rem(lax.axis_index("rows"), 2) == 0
    for half, side in enumerate(sides):
        first, last = side[:16], side[tok - 16 :]
        lanes = slice(half * width, (half + 1) * width)
        near[:, lanes] = jnp.where(even, last.astype(F32), first.astype(F32)).astype(BF16)
        far[:, lanes] = jnp.where(even, first.astype(F32), last.astype(F32)).astype(BF16)
    both = jnp.concatenate([w[0], w[1]], axis=1)
    for strand in range(2):
        side = sides[strand]
        if strand == 1:
            side = low(nn(side, turn[...]))
        source = nn(mover[...], side)
        inverse = lax.rsqrt(jnp.mean(source * source, axis=-1, keepdims=True) + EPSILON)
        rows = low(source * inverse * gains[:1])
        normed[strand] = rows
        out = nn(rows, both)
        lanes = out.shape[1] // 2
        inputs[strand] = low(out[:, :lanes] * valid[...])
        gates[strand] = out[:, lanes:]


def cotangent_kernel(geo, co, cc, cy, cd, gates, valid, turn, mover, outs, moved, gm, dys, scratch):
    tok = geo.tok
    sides = assemble((co, cc, cy, cd), scratch)
    for strand in range(2):
        side = sides[strand]
        if strand == 1:
            side = low(nn(side, turn[...]))
        rows = low(nn(mover[...], side))
        moved[strand] = rows
        grad = nt(rows, outs[0]) * valid[...]
        gm[strand] = grad
        dys[strand] = grad * silu(gates[strand])


def rim_valid(geo, lengths_ref):
    _, offset, length = geo.place(lengths_ref)
    row = iota((32, 1), 0)
    token = jnp.where(row < 16, row - 16, geo.tok + row - 16) + offset
    index = token - offset + lax.axis_index("rows") * geo.tok
    inside = (token >= 0) & (token < geo.window) & (token < length)
    inside = inside & (index >= 0) & (index < geo.tok * geo.rows)
    return jnp.where(inside, 1.0, 0.0)


def fill_padded(padded, main, rims, steps):
    rim = padded.shape[0] // CHUNKS - steps
    rim = rim // 2
    lanes = main.shape[1]
    sub = iota((CHUNKS, lanes), 0)
    padded[rim * CHUNKS : (rim + steps) * CHUNKS] = main
    for k in range(1, rim + 1):
        block = main[(steps - k) * CHUNKS : (steps - k + 1) * CHUNKS]
        moved = pltpu.roll(block, 1, 0)
        edge = jnp.broadcast_to(rims[16 - k : 17 - k], (CHUNKS, lanes))
        padded[(rim - k) * CHUNKS : (rim - k + 1) * CHUNKS] = jnp.where(sub == 0, edge, moved)
    for k in range(rim):
        block = main[k * CHUNKS : (k + 1) * CHUNKS]
        moved = pltpu.roll(block, CHUNKS - 1, 0)
        edge = jnp.broadcast_to(rims[16 + k : 17 + k], (CHUNKS, lanes))
        at = rim + steps + k
        padded[at * CHUNKS : (at + 1) * CHUNKS] = jnp.where(sub == CHUNKS - 1, edge, moved)


def tap_start(tap, taps, flipped):
    return (2 * (taps - 1) - tap if flipped else tap) * CHUNKS


def conv_kernel(
    geo, inputs, near, far, edge, turn, gains, w, select, tiny, after, padded, rims_normed, pre, act, message
):
    tok, steps = geo.tok, geo.steps
    taps = (padded.shape[1] // CHUNKS - steps) // 2 + 1
    lanes = w.shape[2]
    width = w.shape[1]
    even = lax.rem(lax.axis_index("rows"), 2) == 0
    for strand in range(2):
        part = slice(strand * width, (strand + 1) * width)
        one, two = near[:, part].astype(F32), far[:, part].astype(F32)
        source = jnp.concatenate([jnp.where(even, two, one), jnp.where(even, one, two)], axis=0)
        if strand == 1:
            source = nn(low(source), turn[...])
        inverse = lax.rsqrt(jnp.mean(source * source, axis=-1, keepdims=True) + EPSILON)
        rows = low(source * inverse * gains[:1])
        rims_normed[strand] = rows
        edges = low(nn(rows, w[0]) * edge[...]).astype(F32)
        main = inputs[strand].astype(F32)
        fill_padded(padded.at[strand], main, edges, steps)
        total = jnp.zeros((tok, LANES), F32)
        for course in range(2):
            member = 2 * strand + course
            running = jnp.broadcast_to(tiny[8 + course : 9 + course], (tok, lanes))
            for tap in range(taps):
                at = tap_start(tap, taps, FLIPS[member])
                row = course * taps + tap
                running = running + tiny[row : row + 1] * padded[strand, at : at + tok]
            pre[member] = running
            active = low(silu(running))
            act[member] = active
            total = total + nt(active, select[course])
        message[strand] = low(total)


def columns(n):
    return slice(n * LANES, (n + 1) * LANES)


def summary_kernel(
    geo, one, two, act, dys, stw, tiny, table, spread, valid,
    proj, raw, step, drive, chunk_p, chunk_h, chunk_w, wide, near, far, up, down,
):
    tok, steps = geo.tok, geo.steps
    for strand in range(2):
        total = one[strand].astype(F32) + two[strand].astype(F32)
        for course in range(2):
            member = 2 * strand + course
            here = total if course == 0 else pltpu.roll(total, 64, 1)
            rounded = low(here)
            proj[member] = rounded
            rest = pltpu.roll(here - rounded.astype(F32), 64, 1)
            lane = iota(here.shape, 1)
            split = low(jnp.where(lane < 64, here, rest))
            for at in range(0, 2 * N * LANES, 512):
                wide[member, :, at : at + 512] = nn(split, spread[:, at : at + 512])
            step_raw = nn(rounded[:, :R], stw[course]) + tiny[10 + course : 11 + course]
            step_row = softplus(step_raw) * valid[...]
            raw[member] = step_raw
            step[member] = step_row
            drive[member] = step_row * act[member].astype(F32)
    def sweep(member, flipped):
        strand, course = member // 2, lax.rem(member, 2)
        for base in range(0, N, 8):

            def body(k, carry):
                ps, hs, ws = carry
                t = steps - 1 - k if flipped else k
                rows = pl.ds(pl.multiple_of(t * CHUNKS, CHUNKS), CHUNKS)
                s, d, y = step[member, rows], drive[member, rows], dys[strand, rows]
                np_, nh, nw = [], [], []
                for i in range(8):
                    n = base + i
                    decay_here = jnp.exp2(s * table[2 + course, n])
                    p = ps[i] * decay_here
                    np_.append(p)
                    nh.append(hs[i] * decay_here + wide[member, rows, columns(n)] * d)
                    nw.append(ws[i] + p * (wide[member, rows, columns(N + n)] * y))
                return tuple(np_), tuple(nh), tuple(nw)

            zero = jnp.zeros((CHUNKS, LANES), F32)
            start = (tuple([zero + 1.0] * 8), (zero,) * 8, (zero,) * 8)
            ps, hs, ws = lax.fori_loop(0, steps, body, start, unroll=4)
            for i in range(8):
                rows = slice((base + i) * CHUNKS, (base + i + 1) * CHUNKS)
                chunk_p[member, rows] = ps[i]
                chunk_h[member, rows] = hs[i]
                chunk_w[member, rows] = ws[i]

    lax.fori_loop(0, 2, lambda i, c: (sweep(3 * i, False), c)[1], 0)
    lax.fori_loop(0, 2, lambda i, c: (sweep(1 + i, True), c)[1], 0)

    slots = {0: (0, 2), 3: (1, 3), 1: (2, 0), 2: (3, 1)}
    for member in range(4):
        h = jnp.zeros((N, LANES), F32)
        w = jnp.zeros((N, LANES), F32)
        order = list(range(CHUNKS))
        forward = order[::-1] if FLIPS[member] else order
        for j in forward:
            rows = pl.ds(j, N, stride=CHUNKS)
            h = chunk_p[member, rows] * h + chunk_h[member, rows]
        for j in forward[::-1]:
            rows = pl.ds(j, N, stride=CHUNKS)
            w = chunk_p[member, rows] * w + chunk_w[member, rows]
        length = jnp.sum(step[member], axis=0, keepdims=True)
        slot_up, slot_down = slots[member]
        goes_up, goes_down = (w, h) if FLIPS[member] else (h, w)
        up[slot_up * N : (slot_up + 1) * N] = goes_up
        down[slot_down * N : (slot_down + 1) * N] = goes_down
        up[4 * N + slot_up : 4 * N + slot_up + 1] = length
        down[4 * N + slot_down : 4 * N + slot_down + 1] = length
    up[4 * N + 4 :] = jnp.zeros((4, LANES), F32)
    down[4 * N + 4 :] = jnp.zeros((4, LANES), F32)
    if near is not None:
        local = geo.local()
        near[...] = jnp.where(lax.rem(local, 2) == 0, up[...], down[...])
        far[...] = jnp.where(local < 2, up[...], down[...])


UP_MEMBERS = (0, 3, 1, 2)
DOWN_MEMBERS = (1, 2, 0, 3)


def scan_kernel(
    geo, slot_refs, act, proj, raw, step, drive, chunk_p, chunk_h, chunk_w, wide, spread,
    dys, gm, gates, stw, tiny, table, valid,
    mixed, dgate, dact, message, small,
    slots, enter, adjoint, states, quads, out_y, slope_y, pull_y, dproj, dacc,
):
    tok, steps = geo.tok, geo.steps
    count = geo.members
    row = lax.axis_index("rows")
    local = geo.local()
    base_row = row - local
    if len(slot_refs) == 1:
        slots = slot_refs[0]
    else:
        slots[local] = jnp.zeros(slots.shape[1:], F32)
        others = (lax.bitwise_xor(local, 1), lax.rem(local + 2, 4), 3 - local)
        for at, ref in zip(others, slot_refs):
            slots[at] = ref[...]
    dacc[...] = jnp.zeros_like(dacc)

    def fold(ascending, carried):
        members = UP_MEMBERS if ascending else DOWN_MEMBERS
        tables = [tiny[24 + N * (m % 2) : 24 + N * (m % 2) + N] for m in members]

        def one(i, carried):
            k = i if ascending else count - 1 - i
            there = base_row + k
            use = (k < local) if ascending else (k > local)
            use = use & (there >= 0) & (there < geo.rows)
            out = []
            for q in range(4):
                length = slots[k, 4 * N + q : 4 * N + q + 1]
                new = jnp.exp2(tables[q] * length) * carried[q] + slots[k, q * N : (q + 1) * N]
                out.append(jnp.where(use, new, carried[q]))
            return tuple(out)

        return lax.fori_loop(0, count, one, carried)

    zero = (jnp.zeros((N, LANES), F32),) * 4
    from_below = fold(True, zero)
    from_above = fold(False, zero)
    order = list(range(CHUNKS))
    for q in range(4):
        for value, member, js in (
            (from_below[q], UP_MEMBERS[q], order),
            (from_above[q], DOWN_MEMBERS[q], order[::-1]),
        ):
            target, source = (enter, chunk_h) if q < 2 else (adjoint, chunk_w)
            for j in js:
                rows = pl.ds(j, N, stride=CHUNKS)
                target[member, rows] = value
                value = chunk_p[member, rows] * value + source[member, rows]

    def sweep(member, flipped):
        strand, course = member // 2, lax.rem(member, 2)
        states[: N * CHUNKS] = enter[member]

        def ahead(i, carry):
            hs = list(carry)
            kept = []
            for sub in range(2):
                k = 2 * i + sub
                t = steps - 1 - k if flipped else k
                rows = pl.ds(pl.multiple_of(t * CHUNKS, CHUNKS), CHUNKS)
                s, d, y = step[member, rows], drive[member, rows], dys[strand, rows]
                total = jnp.zeros((CHUNKS, LANES), F32)
                products = []
                for n in range(N):
                    hs[n] = hs[n] * jnp.exp2(s * table[2 + course, n]) + wide[member, rows, columns(n)] * d
                    total = total + wide[member, rows, columns(N + n)] * hs[n]
                    products.append(y * hs[n])
                    at = pl.multiple_of(((k + 1) * N + n) * CHUNKS, CHUNKS)
                    states[pl.ds(at, CHUNKS)] = hs[n]
                out_y[member, rows] = total
                kept.append(products)
            pair = steps // 2 - 1 - i if flipped else i
            rows = pl.ds(pl.multiple_of(pair * 16, 16), 16)
            first, second = (kept[1], kept[0]) if flipped else (kept[0], kept[1])
            for n in range(N):
                both = low(jnp.concatenate([first[n], second[n]], axis=0))
                quads[rows, (N + n) * LANES : (N + n + 1) * LANES] = both
            return tuple(hs)

        start = tuple(enter[member, n * CHUNKS : (n + 1) * CHUNKS] for n in range(N))
        lax.fori_loop(0, steps // 2, ahead, start)

        def back(i, carry):
            cs, ds = list(carry[0]), list(carry[1])
            kept = []
            for sub in range(2):
                k = steps - 1 - (2 * i + sub)
                t = steps - 1 - k if flipped else k
                rows = pl.ds(pl.multiple_of(t * CHUNKS, CHUNKS), CHUNKS)
                s, d, y = step[member, rows], drive[member, rows], dys[strand, rows]
                pulled = jnp.zeros((CHUNKS, LANES), F32)
                slope = jnp.zeros((CHUNKS, LANES), F32)
                products = []
                for n in range(N):
                    lam = y * wide[member, rows, columns(N + n)] + cs[n]
                    pulled = pulled + lam * wide[member, rows, columns(n)]
                    products.append(lam * d)
                    cs[n] = lam * jnp.exp2(s * table[2 + course, n])
                    at = pl.multiple_of((k * N + n) * CHUNKS, CHUNKS)
                    u = cs[n] * states[pl.ds(at, CHUNKS)]
                    slope = slope + u * table[course, n]
                    ds[n] = ds[n] + u * s
                slope_y[member, rows] = slope
                pull_y[member, rows] = pulled
                kept.append(products)
            pair = i if flipped else steps // 2 - 1 - i
            rows = pl.ds(pl.multiple_of(pair * 16, 16), 16)
            first, second = (kept[0], kept[1]) if flipped else (kept[1], kept[0])
            for n in range(N):
                both = low(jnp.concatenate([first[n], second[n]], axis=0))
                quads[rows, n * LANES : (n + 1) * LANES] = both
            return tuple(cs), tuple(ds)

        start = tuple(adjoint[member, n * CHUNKS : (n + 1) * CHUNKS] for n in range(N))
        zeros = (jnp.zeros((CHUNKS, LANES), F32),) * N
        _, ds = lax.fori_loop(0, steps // 2, back, (start, zeros))
        for n in range(N):
            rows = slice(n * CHUNKS, (n + 1) * CHUNKS)
            dacc[course, rows] = dacc[course, rows] + ds[n]
        dproj[member] = nt(spread[:64], quads[...])

    lax.fori_loop(0, 2, lambda i, c: (sweep(3 * i, False), c)[1], 0)
    lax.fori_loop(0, 2, lambda i, c: (sweep(1 + i, True), c)[1], 0)

    small[...] = jnp.zeros_like(small)
    for course in range(2):
        for n in range(N):
            total = jnp.sum(dacc[course, n * CHUNKS : (n + 1) * CHUNKS], axis=0, keepdims=True)
            at = 2 * R + course * N + n
            small[at : at + 1] = total * table[course, n, :1]
    for strand in range(2):
        joined = jnp.zeros((tok, LANES), F32)
        grad = dys[strand]
        for course in range(2):
            member = 2 * strand + course
            active = act[member].astype(F32)
            joined = joined + out_y[member] + tiny[12 + course : 13 + course] * active
            raw_grad = slope_y[member] + pull_y[member] * active
            rounded = low(raw_grad * valid[...] * sigmoid(raw[member]))
            dact[member] = pull_y[member] * step[member] + grad * tiny[12 + course : 13 + course]
            rows = slice(course * R, (course + 1) * R)
            small[rows] += tn(proj[member], rounded)[:R]
            at = 2 * R + 2 * N + course
            small[at : at + 1] += jnp.sum(rounded.astype(F32), axis=0, keepdims=True)
            small[at + 2 : at + 3] += jnp.sum(grad * active, axis=0, keepdims=True)
            message[strand, 64 * course : 64 * course + R] = low(nt(stw[course], rounded))
            message[strand, 64 * course + R : 64 * course + 64] = low(dproj[member, R:])
        gate = gates[strand]
        mixed[strand] = low(joined * silu(gate) * valid[...])
        dgate[strand] = low(gm[strand] * joined * silu_slope(gate))


E_ROWS = 608
L_ROWS = 384
GAIN_ROWS = 16


def halves(pack, total, keep, send):
    half = total // 2
    mine = lax.rem(lax.axis_index("rows"), 2)
    if keep.shape[0] >= total:
        keep[:total] = pack[:total]
        send[:half] = jnp.zeros((half, LANES), BF16)
    else:
        keep[:half] = pack[pl.ds(pl.multiple_of(mine * half, 16), half)]
        send[:half] = low(pack[pl.ds(pl.multiple_of((1 - mine) * half, 16), half)])


def dense_kernel(
    geo, mixed, outs, moved, dgate, normed, weights, back, small, kept, sent, keep, send, g_gate, dn_gate, pack
):
    width = weights.shape[1]
    second = lax.axis_index("ch") >= 2
    branches = []
    grad_out = jnp.zeros((LANES, width), F32)
    grad_gate = jnp.zeros(g_gate.shape, F32)
    for strand in range(2):
        branches.append(nn(low(nn(back[...], mixed[strand])), outs[strand]))
        grad_out = grad_out + tn(mixed[strand], moved[strand])
        grad_gate = grad_gate + tn(normed[strand], dgate[strand])
        dn_gate[strand] = nt(low(nn(back[...], dgate[strand])), weights[1 + 2 * strand])
    kept[...] = jnp.where(second, branches[1], branches[0])
    sent[...] = low(jnp.where(second, branches[0], branches[1]))
    g_gate[...] = grad_gate
    pack[:width] = grad_gate
    pack[width : width + LANES] = grad_out[:, :LANES]
    pack[width + LANES : width + 2 * LANES] = grad_out[:, LANES:]
    pack[width + 2 * LANES : width + 2 * LANES + 80] = small[...]
    pack[width + 2 * LANES + 80 :] = jnp.zeros((16, LANES), F32)
    halves(pack, E_ROWS, keep, send)


def conv_back_kernel(
    geo, one, two, act, dact, pre, padded, tiny, select, normed, rims_normed, gains, w, g_gate, valid, edge,
    res_kept, res_got,
    xg, near, far, keep, send, res_own, res_sent,
    pad_grad, pack,
):
    tok, steps = geo.tok, geo.steps
    taps = (padded.shape[1] // CHUNKS - steps) // 2 + 1
    width = w.shape[1]
    even = lax.rem(lax.axis_index("rows"), 2) == 0
    rim = taps - 1
    sub = iota((CHUNKS, LANES), 0)
    pack[...] = jnp.zeros_like(pack)
    grad_select = [jnp.zeros((64, LANES), F32)] * 2
    grad_in = jnp.zeros((width, LANES), F32)
    at_conv = width + LANES - 32
    for strand in range(2):
        pad_grad[...] = jnp.zeros_like(pad_grad)
        rounded = low(one[strand].astype(F32) + two[strand].astype(F32))
        for course in range(2):
            member = 2 * strand + course
            mine = slice(64 * course, 64 * course + 64)
            grad_select[course] = grad_select[course] + nn(rounded[mine], act[member])
            total = dact[member] + tn(rounded, select[course])
            grad = total * silu_slope(pre[member])
            row = at_conv + 8 + course
            pack[row : row + 1] += jnp.sum(grad, axis=0, keepdims=True)
            for tap in range(taps):
                at = tap_start(tap, taps, FLIPS[member])
                row = at_conv + course * taps + tap
                pack[row : row + 1] += jnp.sum(grad * padded[strand, at : at + tok], axis=0, keepdims=True)
                at_tap = course * taps + tap
                pad_grad[at : at + tok] += tiny[at_tap : at_tap + 1] * grad
        before = [jnp.zeros((1, LANES), F32)] * (16 - rim)
        after = []
        for k in range(rim, 0, -1):
            block = pad_grad[(rim - k) * CHUNKS : (rim - k + 1) * CHUNKS]
            before.append(block[:1])
            moved = jnp.where(sub == CHUNKS - 1, 0.0, pltpu.roll(block, CHUNKS - 1, 0))
            at = (rim + steps - k) * CHUNKS
            pad_grad[at : at + CHUNKS] += moved
        for k in range(rim):
            at = (rim + steps + k) * CHUNKS
            block = pad_grad[at : at + CHUNKS]
            after.append(block[CHUNKS - 1 :])
            moved = jnp.where(sub == 0, 0.0, pltpu.roll(block, 1, 0))
            at = (rim + k) * CHUNKS
            pad_grad[at : at + CHUNKS] += moved
        after += [jnp.zeros((1, LANES), F32)] * (16 - rim)
        rims = jnp.concatenate(before + after, axis=0) * edge[...]
        main = pad_grad[rim * CHUNKS : (rim + steps) * CHUNKS]
        xg[strand] = main
        grad_in = grad_in + tn(normed[strand], low(main * valid[...])) + tn(rims_normed[strand], low(rims))
        near[strand] = jnp.where(even, rims[16:], rims[:16])
        far[strand] = jnp.where(even, rims[:16], rims[16:])
    pack[:width] = grad_in
    amount = LANES // 2 - 16
    for course in range(2):
        pack[width + course * amount : width + (course + 1) * amount] = grad_select[course][:amount]
    halves(pack, L_ROWS, keep, send)
    product = grad_in * w[0].astype(F32) + g_gate[...] * w[1].astype(F32)
    high = low(product)
    ones = jnp.ones((8, LANES), BF16)
    gain_part = (nt(ones, high) + nt(ones, low(product - high.astype(F32)))) / gains[:1]
    at = keep.shape[0] - GAIN_ROWS
    keep[at : at + 8] = gain_part[:, :LANES]
    keep[at + 8 :] = gain_part[:, LANES:]
    at = send.shape[0] - GAIN_ROWS
    send[at:] = low(jnp.concatenate([gain_part[:, :LANES], gain_part[:, LANES:]], axis=0))
    total = res_kept[...] + res_got[...].astype(F32)
    odd = lax.rem(lax.axis_index("ch"), 2) == 1
    res_own[...] = jnp.where(odd, total[:, LANES:], total[:, :LANES])
    res_sent[...] = low(jnp.where(odd, total[:, :LANES], total[:, LANES:]))


def normed_back_kernel(
    geo, xg, near, far, dn_gate, weights, valid, back, hidden, res_own, res_got, kept, sent, result
):
    tok, steps = geo.tok, geo.steps
    even = lax.rem(lax.axis_index("rows"), 2) == 0
    second = lax.axis_index("ch") >= 2
    row = iota((tok, LANES), 0)
    token = (row % CHUNKS) * steps + row // CHUNKS
    grads = []
    for strand in range(2):
        one, two = near[strand], far[strand]
        ahead = jnp.where(even, two, one)
        behind = jnp.where(even, one, two)
        total = xg[strand]
        for k in range(3):
            total = total + jnp.where(token == k, ahead[k : k + 1], 0.0)
            total = total + jnp.where(token == tok - 1 - k, behind[15 - k : 16 - k], 0.0)
        rounded = low(total * valid[...])
        grads.append(nt(low(nn(back[...], rounded)), weights[2 * strand]) + dn_gate[strand])
    kept[...] = jnp.where(second, grads[1], grads[0])
    sent[...] = low(jnp.where(second, grads[0], grads[1]))
    out = hidden[...].astype(F32) + res_own[...] + res_got[...].astype(F32)
    result[...] = low(out)


def finish_kernel(geo, one, two, xo, xc, gains, cot, input_grad):
    mine = lax.axis_index("ch")
    odd = lax.rem(mine, 2) == 1
    a, b = xo[...].astype(F32), xc[...].astype(F32)
    source = jnp.concatenate([jnp.where(odd, b, a), jnp.where(odd, a, b)], axis=1)
    inverse = lax.rsqrt(jnp.mean(source * source, axis=-1, keepdims=True) + EPSILON)
    unit = source * inverse
    here = jnp.where(mine >= 2, gains[1:], gains[:1])
    scaled = (one[...].astype(F32) + two[...].astype(F32)) * here
    back = inverse * (scaled - unit * jnp.mean(scaled * unit, axis=-1, keepdims=True))
    input_grad[...] = cot[...].astype(F32) + jnp.where(odd, back[:, LANES:], back[:, :LANES])


def unpack_kernel(e_parts, l_parts, gain_sum, in_g, out_g, sel_g, cw_g, cb_g, stw_g, stb_g, decay_g, skip_g, gain_g, e_pack, l_pack):
    mine = lax.rem(lax.axis_index("rows"), 2)
    for parts, pack in ((e_parts, e_pack), (l_parts, l_pack)):
        total = pack.shape[0]
        half = total // 2
        if len(parts) == 1:
            pack[...] = parts[0][:total].astype(F32)
        else:
            pack[pl.ds(pl.multiple_of(mine * half, 16), half)] = parts[0][:half].astype(F32)
            pack[pl.ds(pl.multiple_of((1 - mine) * half, 16), half)] = parts[1][:half].astype(F32)
    width = in_g.shape[1]
    in_g[0] = l_pack[:width]
    in_g[1] = e_pack[:width]
    out_g[:, :LANES] = e_pack[width : width + LANES]
    out_g[:, LANES:] = e_pack[width + LANES : width + 2 * LANES]
    amount = sel_g.shape[1]
    for course in range(2):
        sel_g[course] = l_pack[width + course * amount : width + (course + 1) * amount]
    at = width + 2 * amount
    taps = cw_g.shape[1]
    for course in range(2):
        cw_g[course] = l_pack[at + course * taps : at + (course + 1) * taps]
    cb_g[...] = l_pack[at + 2 * taps : at + 2 * taps + 2]
    at = width + 2 * LANES
    for course in range(2):
        stw_g[course] = e_pack[at + course * R : at + (course + 1) * R]
        decay_g[course] = e_pack[at + 2 * R + course * N : at + 2 * R + (course + 1) * N]
    at = at + 2 * R + 2 * N
    stb_g[...] = e_pack[at : at + 2]
    skip_g[...] = e_pack[at + 2 : at + 4]
    gain_g[:, :LANES] = gain_sum[:1].astype(F32)
    gain_g[:, LANES:] = gain_sum[8:9].astype(F32)


def swap(value, axis, distance):
    count = lax.axis_size(axis)
    return lax.ppermute(value, axis, [(i, i ^ distance) for i in range(count)])


def gather_channels(value):
    across = swap(value, "ch", 2)
    return value, swap(value, "ch", 1), across, swap(across, "ch", 1)


def partner_sum(value):
    joined = low(value.astype(F32) + swap(value, "ch", 2).astype(F32))
    return joined, swap(joined, "ch", 1)


def on_device(
    hidden_in, lengths, norm_gain, in_weight, conv_weight, conv_bias, select_weight,
    step_weight, step_bias, decay_log, skip_gain, out_weight, cotangent,
):
    tok = hidden_in.shape[0]
    rows = lax.axis_size("rows")
    geo = Geometry(tok, rows)
    steps = geo.steps
    width = in_weight.shape[1]
    gain = norm_gain[None, :]
    small_mesh = geo.members == 4 and rows == 8
    padded_rows = (steps + 2 * (conv_weight.shape[1] - 1)) * CHUNKS

    def kernel(f):
        return functools.partial(f, geo)

    def lifted(f, first, amount):
        def body(*refs):
            return f(*refs[:first], refs[first : first + amount], *refs[first + amount :])

        return body

    vm = pltpu.VMEM
    strands = ((2, tok, LANES), F32)
    strands_low = ((2, tok, LANES), BF16)
    members = ((4, tok, LANES), F32)
    members_low = ((4, tok, LANES), BF16)
    chunked = ((4, N * CHUNKS, LANES), F32)
    summary = ((4 * N + 8, LANES), F32)
    full = ((tok, width), F32)
    full_low = ((tok, width), BF16)

    x_parts = gather_channels(hidden_in)
    x_own, c_own, valid, edge, turn, mover, back, gains, weights, outs, select, table, spread, tiny, stw = run(
        kernel(prepare_kernel),
        [
            ((tok, LANES), BF16),
            ((tok, LANES), BF16),
            ((tok, LANES), F32),
            ((32, LANES), F32),
            ((width, width), BF16),
            ((tok, tok), BF16),
            ((tok, tok), BF16),
            ((2, width), F32),
            ((4, width, LANES), BF16),
            ((2, LANES, width), BF16),
            ((2, LANES, LANES), BF16),
            ((4, N, CHUNKS, LANES), F32),
            ((LANES, 2 * N * LANES), BF16),
            ((24 + 2 * N, LANES), F32),
            (step_weight.shape, BF16),
        ],
        lengths, hidden_in, cotangent, in_weight, out_weight, step_weight, gain, conv_weight, conv_bias,
        jnp.swapaxes(select_weight, 1, 2), step_bias, decay_log, skip_gain,
        anywhere=13,
        scratch=[
            pltpu.SMEM(lengths.shape, jnp.int32),
            vm(gain.shape, F32),
            vm(conv_weight.shape, F32),
            vm(conv_bias.shape, F32),
            vm((2, select_weight.shape[2], LANES), BF16),
            vm(step_bias.shape, F32),
            vm(decay_log.shape, F32),
            vm(skip_gain.shape, F32),
            pltpu.SemaphoreType.DMA((13,)),
        ],
        name="prepare", micros=2,
    )
    cot, x_across = lax.optimization_barrier((cotangent, x_parts[2]))
    x_parts = (x_own, x_parts[1], x_across, x_parts[3])
    c_parts = (c_own,) + gather_channels(cot)[1:]

    normed, inputs, gates, near, far = run(
        kernel(project_kernel),
        [((2, tok, width), BF16), strands_low, strands, ((16, 2 * width), BF16), ((16, 2 * width), BF16)],
        *x_parts, valid, turn, mover, gains, weights,
        scratch=[vm((4, tok, LANES), BF16)], name="project",
    )
    near = lax.ppermute(near, "rows", geo.near())
    far = lax.ppermute(far, "rows", geo.far())
    moved, gm, dys = run(
        kernel(cotangent_kernel),
        [((2, tok, width), BF16), strands, strands],
        *c_parts, gates, valid, turn, mover, outs,
        scratch=[vm((4, tok, LANES), BF16)], name="cotangents", micros=1,
    )
    padded, rims_normed, pre, act, message = run(
        kernel(conv_kernel),
        [((2, padded_rows, LANES), F32), ((2, 32, width), BF16), members, members_low, strands_low],
        inputs, near, far, edge, turn, gains, weights, select, tiny, dys,
        name="conv",
    )
    one, two = partner_sum(message)
    shapes = [members_low, members, members, members, chunked, chunked, chunked]
    shapes += [((4, tok, 2 * N * LANES), F32)]

    def summarise(*refs):
        if small_mesh:
            summary_kernel(geo, *refs)
        else:
            summary_kernel(geo, *refs[:17], None, None, *refs[17:])

    got = run(
        summarise, shapes + [summary, summary],
        one, two, act, dys, stw, tiny, table, spread, valid,
        scratch=[vm(summary[0], F32), vm(summary[0], F32)] if small_mesh else (), name="summary", micros=10,
    )
    proj, raw, step, drive, chunk_p, chunk_h, chunk_w, wide = got[:8]
    if small_mesh:
        slots = (
            lax.ppermute(got[8], "rows", geo.near()),
            lax.ppermute(got[9], "rows", geo.across()),
            lax.ppermute(got[9], "rows", geo.far()),
        )
        slot_scratch = vm((4,) + summary[0], F32)
    else:
        up, down = lax.all_gather(got[8], "rows"), lax.all_gather(got[9], "rows")
        place = lax.axis_index("rows")
        index = place - geo.local() + jnp.arange(geo.members)
        inside = jnp.clip(index, 0, rows - 1)
        slots = (jnp.where((index < place)[:, None, None], up[inside], down[inside]),)
        slot_scratch = vm((8, LANES), F32)
    mixed, dgate, dact, message, small = run(
        lifted(kernel(scan_kernel), 0, len(slots)),
        [strands_low, strands_low, members, ((2, LANES, tok), BF16), ((80, LANES), F32)],
        *slots, act, proj, raw, step, drive, chunk_p, chunk_h, chunk_w, wide, spread,
        dys, gm, gates, stw, tiny, table, valid,
        scratch=[
            slot_scratch,
            vm(chunked[0], F32),
            vm(chunked[0], F32),
            vm(((steps + 1) * N * CHUNKS, LANES), F32),
            vm((tok, 2 * N * LANES), BF16),
            vm(members[0], F32),
            vm(members[0], F32),
            vm(members[0], F32),
            vm((4, 64, tok), F32),
            vm((2, N * CHUNKS, LANES), F32),
        ],
        name="scan", micros=16,
    )
    one, two = partner_sum(message)
    e_half = E_ROWS // 2
    l_half = L_ROWS // 2 + GAIN_ROWS
    res_kept, res_sent, e_keep, e_send, g_gate, dn_gate = run(
        kernel(dense_kernel),
        [
            full,
            full_low,
            ((e_half if small_mesh else E_ROWS, LANES), F32),
            ((e_half, LANES), BF16),
            ((width, LANES), F32),
            ((2, tok, width), F32),
        ],
        mixed, outs, moved, dgate, normed, weights, back, small,
        scratch=[vm((E_ROWS, LANES), F32)], name="dense",
    )
    res_got = swap(res_sent, "ch", 2)
    if small_mesh:
        e_sum = low(e_keep + swap(e_send, "rows", 1).astype(F32))
    xg, near, far, l_keep, l_send, res_own, res_sent = run(
        kernel(conv_back_kernel),
        [
            strands,
            ((2, 16, LANES), F32),
            ((2, 16, LANES), F32),
            ((l_half if small_mesh else L_ROWS + GAIN_ROWS, LANES), F32),
            ((l_half, LANES), BF16),
            ((tok, LANES), F32),
            ((tok, LANES), BF16),
        ],
        one, two, act, dact, pre, padded, tiny, select, normed, rims_normed, gains, weights, g_gate, valid, edge,
        res_kept, res_got,
        scratch=[vm((padded_rows, LANES), F32), vm((L_ROWS, LANES), F32)],
        name="conv_back",
    )
    near = lax.ppermute(near, "rows", geo.near())
    if small_mesh:
        l_sum = low(l_keep + swap(l_send, "rows", 1).astype(F32))
        e_sum = low(e_sum.astype(F32) + swap(e_sum, "rows", 2).astype(F32))
    far = lax.ppermute(far, "rows", geo.far())
    res_got = swap(res_sent, "ch", 1)
    dn_kept, dn_sent, result = run(
        kernel(normed_back_kernel),
        [full, full_low, ((tok, LANES), BF16)],
        xg, near, far, dn_gate, weights, valid, back, x_own, res_own, res_got,
        name="normed_back",
    )
    dn_got = swap(dn_sent, "ch", 2)
    dn = low(dn_kept + dn_got.astype(F32))
    input_grad = run(
        kernel(finish_kernel), ((tok, LANES), F32),
        dn, swap(dn, "ch", 1), x_parts[0], x_parts[1], gains, c_own, name="finish",
    )
    if small_mesh:
        l_sum = low(l_sum.astype(F32) + swap(l_sum, "rows", 2).astype(F32))
        e_sum = low(e_sum.astype(F32) + swap(e_sum, "rows", 4).astype(F32))
        l_sum = low(l_sum.astype(F32) + swap(l_sum, "rows", 4).astype(F32))
        e_parts = (e_sum, swap(e_sum, "rows", 1))
        l_parts = (l_sum, swap(l_sum, "rows", 1))
        gain_part = l_sum[l_half - GAIN_ROWS :].astype(F32)
        gain_part = gain_part + swap(gain_part, "ch", 2)
        gain_part = gain_part + swap(gain_part, "ch", 1)
    else:
        e_parts = (lax.psum(e_keep, "rows"),)
        l_parts = (lax.psum(l_keep, "rows"),)
        gain_part = lax.psum(l_parts[0][L_ROWS:], "ch")

    def unpack(*refs):
        k = len(e_parts)
        unpack_kernel(refs[:k], refs[k : 2 * k], *refs[2 * k :])

    got = run(
        unpack,
        [
            (in_weight.shape, F32),
            (out_weight.shape, F32),
            (jnp.swapaxes(select_weight, 1, 2).shape, F32),
            (conv_weight.shape, F32),
            (conv_bias.shape, F32),
            (step_weight.shape, F32),
            (step_bias.shape, F32),
            (decay_log.shape, F32),
            (skip_gain.shape, F32),
            ((1, width), F32),
        ],
        *e_parts, *l_parts, gain_part,
        scratch=[vm((E_ROWS, LANES), F32), vm((L_ROWS, LANES), F32)], name="unpack",
    )
    in_g, out_g, sel_g, cw_g, cb_g, stw_g, stb_g, decay_g, skip_g, gain_g = got
    return (
        result, input_grad, gain_g[0], in_g, cw_g, cb_g, jnp.swapaxes(sel_g, 1, 2), stw_g, stb_g, decay_g, skip_g, out_g,
    )


def solution(mesh):
    lanes = P(None, None, "ch")
    pair = P(None, "ch")
    columns = P(None, "ch", None)
    tokens = P("rows", "ch")
    return jax.shard_map(
        on_device,
        mesh=mesh,
        in_specs=(
            tokens, P(), P(), lanes, lanes, pair, columns, lanes, pair, lanes, pair, P("ch", None), tokens,
        ),
        out_specs=(
            tokens, tokens, P(), lanes, lanes, pair, columns, lanes, pair, lanes, pair, P("ch", None),
        ),
        check_vma=False,
    )
```

```python
import functools

import jax
import jax.numpy as jnp
from jax import lax
from jax.experimental import pallas as pl
from jax.experimental.pallas import tpu as pltpu
from jax.sharding import PartitionSpec as P


N = 16
R = 16
WINDOW = 16384
LANES = 128
CHUNKS = 8
EPSILON = 1e-06
LOG2E = 1.4426950408889634
F32 = jnp.float32
BF16 = jnp.bfloat16
VM = pl.BlockSpec(memory_space=pltpu.VMEM)
FLIPS = (False, True, True, False)


def nn(left, right):
    return lax.dot_general(left, right, (((1,), (0,)), ((), ())), preferred_element_type=F32)


def nt(left, right):
    return lax.dot_general(left, right, (((1,), (1,)), ((), ())), preferred_element_type=F32)


def tn(left, right):
    return lax.dot_general(left, right, (((0,), (0,)), ((), ())), preferred_element_type=F32)


def iota(shape, dim):
    return lax.broadcasted_iota(jnp.int32, shape, dim)


def one_hot(mask):
    return jnp.where(mask, 1.0, 0.0).astype(BF16)


def permuter(tok):
    steps = tok // CHUNKS
    row, col = iota((tok, tok), 0), iota((tok, tok), 1)
    return one_hot((row % CHUNKS) * steps + row // CHUNKS == col)


def unpermuter(tok):
    steps = tok // CHUNKS
    row, col = iota((tok, tok), 0), iota((tok, tok), 1)
    return one_hot((col % CHUNKS) * steps + col // CHUNKS == row)


def mirror(width):
    return one_hot(iota((width, width), 0) + iota((width, width), 1) == width - 1)


def sigmoid(v):
    return 1.0 / (1.0 + jnp.exp(-v))


def silu(v):
    return v * sigmoid(v)


def silu_slope(v):
    logistic = sigmoid(v)
    return logistic * (1.0 + v * (1.0 - logistic))


def softplus(v):
    return jnp.maximum(v, 0.0) + jnp.log1p(jnp.exp(-jnp.abs(v)))


def low(v):
    return v.astype(BF16)


class Geometry:
    def __init__(self, tok, rows):
        self.tok = tok
        self.rows = rows
        self.window = min(WINDOW, tok * rows // 2)
        self.members = self.window // tok
        self.steps = tok // CHUNKS

    def place(self, lengths_ref):
        row = lax.axis_index("rows")
        shifted = row * self.tok + self.window // 2
        offset = lax.rem(shifted, self.window)
        length = lengths_ref[lax.div(shifted, self.window)]
        return row, offset, length

    def valid(self, lengths_ref):
        _, offset, length = self.place(lengths_ref)
        row = iota((self.tok, 1), 0)
        token = (row % CHUNKS) * self.steps + row // CHUNKS
        return jnp.where(offset + token < length, 1.0, 0.0)

    def local(self):
        row = lax.axis_index("rows")
        return lax.rem(row + self.members // 2, self.members)

    def near(self):
        return [(i, i ^ 1) for i in range(self.rows)]

    def far(self):
        if self.members == 4:
            return self.swaps(lambda k: 3 - k)
        out = []
        for i in range(1, self.rows, 2):
            out += [(i, (i + 1) % self.rows), ((i + 1) % self.rows, i)]
        return out

    def across(self):
        return self.swaps(lambda k: (k + 2) % 4)

    def swaps(self, other):
        out = []
        for i in range(self.rows):
            local = (i + 2) % 4
            j = i - local + other(local)
            out.append((i, j if 0 <= j < self.rows else i ^ 1))
        return out


def run(kernel, outs, *args, anywhere=0, scratch=(), micros=1, limit=8):
    single = isinstance(outs, tuple)
    shapes = [outs] if single else list(outs)
    args = [pltpu.with_memory_space_constraint(a, pltpu.HBM) for a in args[:anywhere]] + list(args[anywhere:])
    call = pl.pallas_call(
        kernel,
        out_shape=[jax.ShapeDtypeStruct(s, d) for s, d in shapes],
        in_specs=[pl.BlockSpec(memory_space=pltpu.HBM)] * anywhere + [VM] * (len(args) - anywhere),
        out_specs=[VM] * len(shapes),
        scratch_shapes=list(scratch),
        compiler_params=pltpu.CompilerParams(vmem_limit_bytes=limit * 1024 * 1024),
        cost_estimate=pl.CostEstimate(flops=0, bytes_accessed=int(micros * 3.0e6), transcendentals=0),
    )
    got = call(*args)
    return got[0] if single else got


def assemble(refs, scratch):
    mine = lax.axis_index("ch")
    for distance, ref in enumerate(refs):
        scratch[lax.bitwise_xor(mine, distance)] = ref[...]
    return (
        jnp.concatenate([scratch[0], scratch[1]], axis=1),
        jnp.concatenate([scratch[2], scratch[3]], axis=1),
    )


def prepare_kernel(
    geo, lengths_in, x_in, c_in, w_in, ow_in, stw_in, gain_in, cw_in, cb_in, sw_in, stb_in, decay_in, skip_in,
    x_out, c_out, valid, edge, turn, mover, back, gains, weights, outs, select, table, spread, tiny, stw,
    lengths, gain, cw, cb, sw, stb, decay, skip, sems,
):
    pairs = (
        (lengths_in, lengths), (w_in, weights.at[0:2]), (ow_in, outs.at[0]), (stw_in, stw), (gain_in, gain),
        (cw_in, cw), (cb_in, cb), (sw_in, sw), (stb_in, stb), (decay_in, decay), (skip_in, skip),
        (x_in, x_out), (c_in, c_out),
    )
    copies = [pltpu.make_async_copy(source, target, sems.at[i]) for i, (source, target) in enumerate(pairs)]
    for copy in copies:
        copy.start()
    tok = geo.tok
    width = turn.shape[0]
    flip = mirror(width)
    turn[...] = flip
    mover[...] = permuter(tok)
    back[...] = unpermuter(tok)
    for at in range(0, 2 * N):
        key = iota((LANES, LANES), 0) % 64
        spread[:, at * LANES : (at + 1) * LANES] = one_hot(key == R + at)
    select[...] = jnp.zeros_like(select)
    tiny[...] = jnp.zeros_like(tiny)
    for copy in copies:
        copy.wait()
    valid[...] = jnp.broadcast_to(geo.valid(lengths), valid.shape)
    edge[...] = jnp.broadcast_to(rim_valid(geo, lengths), edge.shape)
    plain = jnp.broadcast_to(gain[...], (8, width))
    high = low(plain)
    rest = plain - high.astype(F32)
    middle = low(rest)
    turned = nn(high, flip) + nn(middle, flip) + nn(low(rest - middle.astype(F32)), flip)
    gains[:1] = gain[...]
    gains[1:] = turned[:1]
    for k in range(2):
        weights[2 + k] = low(nn(flip, weights[k]))
    outs[1] = low(nn(outs[0], flip))
    amount = sw.shape[1]
    for course in range(2):
        select[course, 64 * course : 64 * course + amount] = sw[course]
        natural = -jnp.exp(decay[course])
        for n in range(N):
            level = jnp.broadcast_to(natural[n : n + 1], (CHUNKS, LANES))
            table[course, n] = level
            table[2 + course, n] = level * LOG2E
    taps = cw.shape[1]
    for course in range(2):
        tiny[course * taps : (course + 1) * taps] = cw[course]
        tiny[24 + course * N : 24 + (course + 1) * N] = -LOG2E * jnp.exp(decay[course])
    tiny[8:10] = cb[...]
    tiny[10:12] = stb[...]
    tiny[12:14] = skip[...]


def project_kernel(geo, xo, xc, xy, xd, valid, turn, mover, gains, w, normed, inputs, gates, near, far, scratch):
    tok = geo.tok
    width = w.shape[1]
    sides = assemble((xo, xc, xy, xd), scratch)
    even = lax.rem(lax.axis_index("rows"), 2) == 0
    for half, side in enumerate(sides):
        first, last = side[:16], side[tok - 16 :]
        lanes = slice(half * width, (half + 1) * width)
        near[:, lanes] = jnp.where(even, last.astype(F32), first.astype(F32)).astype(BF16)
        far[:, lanes] = jnp.where(even, first.astype(F32), last.astype(F32)).astype(BF16)
    both = jnp.concatenate([w[0], w[1]], axis=1)
    for strand in range(2):
        side = sides[strand]
        if strand == 1:
            side = low(nn(side, turn[...]))
        source = nn(mover[...], side)
        inverse = lax.rsqrt(jnp.mean(source * source, axis=-1, keepdims=True) + EPSILON)
        rows = low(source * inverse * gains[:1])
        normed[strand] = rows
        out = nn(rows, both)
        lanes = out.shape[1] // 2
        inputs[strand] = low(out[:, :lanes] * valid[...])
        gates[strand] = out[:, lanes:]


def cotangent_kernel(geo, co, cc, cy, cd, gates, valid, turn, mover, outs, moved, gm, dys, scratch):
    sides = assemble((co, cc, cy, cd), scratch)
    for strand in range(2):
        side = sides[strand]
        if strand == 1:
            side = low(nn(side, turn[...]))
        rows = low(nn(mover[...], side))
        moved[strand] = rows
        grad = nt(rows, outs[0]) * valid[...]
        gm[strand] = grad
        dys[strand] = grad * silu(gates[strand])


def rim_valid(geo, lengths_ref):
    _, offset, length = geo.place(lengths_ref)
    row = iota((32, 1), 0)
    token = jnp.where(row < 16, row - 16, geo.tok + row - 16) + offset
    index = token - offset + lax.axis_index("rows") * geo.tok
    inside = (token >= 0) & (token < geo.window) & (token < length)
    inside = inside & (index >= 0) & (index < geo.tok * geo.rows)
    return jnp.where(inside, 1.0, 0.0)


def fill_padded(padded, main, rims, steps):
    rim = padded.shape[0] // CHUNKS - steps
    rim = rim // 2
    lanes = main.shape[1]
    sub = iota((CHUNKS, lanes), 0)
    padded[rim * CHUNKS : (rim + steps) * CHUNKS] = main
    for k in range(1, rim + 1):
        block = main[(steps - k) * CHUNKS : (steps - k + 1) * CHUNKS]
        moved = pltpu.roll(block, 1, 0)
        edge = jnp.broadcast_to(rims[16 - k : 17 - k], (CHUNKS, lanes))
        padded[(rim - k) * CHUNKS : (rim - k + 1) * CHUNKS] = jnp.where(sub == 0, edge, moved)
    for k in range(rim):
        block = main[k * CHUNKS : (k + 1) * CHUNKS]
        moved = pltpu.roll(block, CHUNKS - 1, 0)
        edge = jnp.broadcast_to(rims[16 + k : 17 + k], (CHUNKS, lanes))
        at = rim + steps + k
        padded[at * CHUNKS : (at + 1) * CHUNKS] = jnp.where(sub == CHUNKS - 1, edge, moved)


def tap_start(tap, taps, flipped):
    return (2 * (taps - 1) - tap if flipped else tap) * CHUNKS


def conv_kernel(
    geo, inputs, near, far, edge, turn, gains, w, select, tiny, after, padded, rims_normed, pre, act, message
):
    tok, steps = geo.tok, geo.steps
    taps = (padded.shape[1] // CHUNKS - steps) // 2 + 1
    lanes = w.shape[2]
    width = w.shape[1]
    even = lax.rem(lax.axis_index("rows"), 2) == 0
    for strand in range(2):
        part = slice(strand * width, (strand + 1) * width)
        one, two = near[:, part].astype(F32), far[:, part].astype(F32)
        source = jnp.concatenate([jnp.where(even, two, one), jnp.where(even, one, two)], axis=0)
        if strand == 1:
            source = nn(low(source), turn[...])
        inverse = lax.rsqrt(jnp.mean(source * source, axis=-1, keepdims=True) + EPSILON)
        rows = low(source * inverse * gains[:1])
        rims_normed[strand] = rows
        edges = low(nn(rows, w[0]) * edge[...]).astype(F32)
        main = inputs[strand].astype(F32)
        fill_padded(padded.at[strand], main, edges, steps)
        total = jnp.zeros((tok, LANES), F32)
        for course in range(2):
            member = 2 * strand + course
            running = jnp.broadcast_to(tiny[8 + course : 9 + course], (tok, lanes))
            for tap in range(taps):
                at = tap_start(tap, taps, FLIPS[member])
                row = course * taps + tap
                running = running + tiny[row : row + 1] * padded[strand, at : at + tok]
            pre[member] = running
            active = low(silu(running))
            act[member] = active
            total = total + nt(active, select[course])
        message[strand] = low(total)


def columns(n):
    return slice(n * LANES, (n + 1) * LANES)


def summary_kernel(
    geo, one, two, act, dys, stw, tiny, table, spread, valid,
    proj, raw, step, drive, chunk_p, chunk_h, chunk_w, wide, near, far, up, down,
):
    steps = geo.steps
    for strand in range(2):
        total = one[strand].astype(F32) + two[strand].astype(F32)
        for course in range(2):
            member = 2 * strand + course
            here = total if course == 0 else pltpu.roll(total, 64, 1)
            rounded = low(here)
            proj[member] = rounded
            rest = pltpu.roll(here - rounded.astype(F32), 64, 1)
            lane = iota(here.shape, 1)
            split = low(jnp.where(lane < 64, here, rest))
            for at in range(0, 2 * N * LANES, 512):
                wide[member, :, at : at + 512] = nn(split, spread[:, at : at + 512])
            step_raw = nn(rounded[:, :R], stw[course]) + tiny[10 + course : 11 + course]
            step_row = softplus(step_raw) * valid[...]
            raw[member] = step_raw
            step[member] = step_row
            drive[member] = step_row * act[member].astype(F32)

    def sweep(member, flipped):
        strand, course = member // 2, lax.rem(member, 2)
        for base in range(0, N, 8):

            def body(k, carry):
                ps, hs, ws = carry
                t = steps - 1 - k if flipped else k
                rows = pl.ds(pl.multiple_of(t * CHUNKS, CHUNKS), CHUNKS)
                s, d, y = step[member, rows], drive[member, rows], dys[strand, rows]
                np_, nh, nw = [], [], []
                for i in range(8):
                    n = base + i
                    decay_here = jnp.exp2(s * table[2 + course, n])
                    p = ps[i] * decay_here
                    np_.append(p)
                    nh.append(hs[i] * decay_here + wide[member, rows, columns(n)] * d)
                    nw.append(ws[i] + p * (wide[member, rows, columns(N + n)] * y))
                return tuple(np_), tuple(nh), tuple(nw)

            zero = jnp.zeros((CHUNKS, LANES), F32)
            start = (tuple([zero + 1.0] * 8), (zero,) * 8, (zero,) * 8)
            ps, hs, ws = lax.fori_loop(0, steps, body, start, unroll=4)
            for i in range(8):
                rows = slice((base + i) * CHUNKS, (base + i + 1) * CHUNKS)
                chunk_p[member, rows] = ps[i]
                chunk_h[member, rows] = hs[i]
                chunk_w[member, rows] = ws[i]

    lax.fori_loop(0, 2, lambda i, c: (sweep(3 * i, False), c)[1], 0)
    lax.fori_loop(0, 2, lambda i, c: (sweep(1 + i, True), c)[1], 0)

    slots = {0: (0, 2), 3: (1, 3), 1: (2, 0), 2: (3, 1)}
    for member in range(4):
        h = jnp.zeros((N, LANES), F32)
        w = jnp.zeros((N, LANES), F32)
        order = list(range(CHUNKS))
        forward = order[::-1] if FLIPS[member] else order
        for j in forward:
            rows = pl.ds(j, N, stride=CHUNKS)
            h = chunk_p[member, rows] * h + chunk_h[member, rows]
        for j in forward[::-1]:
            rows = pl.ds(j, N, stride=CHUNKS)
            w = chunk_p[member, rows] * w + chunk_w[member, rows]
        length = jnp.sum(step[member], axis=0, keepdims=True)
        slot_up, slot_down = slots[member]
        goes_up, goes_down = (w, h) if FLIPS[member] else (h, w)
        up[slot_up * N : (slot_up + 1) * N] = goes_up
        down[slot_down * N : (slot_down + 1) * N] = goes_down
        up[4 * N + slot_up : 4 * N + slot_up + 1] = length
        down[4 * N + slot_down : 4 * N + slot_down + 1] = length
    up[4 * N + 4 :] = jnp.zeros((4, LANES), F32)
    down[4 * N + 4 :] = jnp.zeros((4, LANES), F32)
    if near is not None:
        local = geo.local()
        near[...] = jnp.where(lax.rem(local, 2) == 0, up[...], down[...])
        far[...] = jnp.where(local < 2, up[...], down[...])


UP_MEMBERS = (0, 3, 1, 2)
DOWN_MEMBERS = (1, 2, 0, 3)


def scan_kernel(
    geo, slot_refs, act, proj, raw, step, drive, chunk_p, chunk_h, chunk_w, wide, spread,
    dys, gm, gates, stw, tiny, table, valid,
    mixed, dgate, dact, message, small,
    slots, enter, adjoint, states, quads, out_y, slope_y, pull_y, dproj, dacc,
):
    tok, steps = geo.tok, geo.steps
    count = geo.members
    row = lax.axis_index("rows")
    local = geo.local()
    base_row = row - local
    if len(slot_refs) == 1:
        slots = slot_refs[0]
    else:
        slots[local] = jnp.zeros(slots.shape[1:], F32)
        others = (lax.bitwise_xor(local, 1), lax.rem(local + 2, 4), 3 - local)
        for at, ref in zip(others, slot_refs):
            slots[at] = ref[...]
    dacc[...] = jnp.zeros_like(dacc)

    def fold(ascending, carried):
        members = UP_MEMBERS if ascending else DOWN_MEMBERS
        tables = [tiny[24 + N * (m % 2) : 24 + N * (m % 2) + N] for m in members]

        def one(i, carried):
            k = i if ascending else count - 1 - i
            there = base_row + k
            use = (k < local) if ascending else (k > local)
            use = use & (there >= 0) & (there < geo.rows)
            out = []
            for q in range(4):
                length = slots[k, 4 * N + q : 4 * N + q + 1]
                new = jnp.exp2(tables[q] * length) * carried[q] + slots[k, q * N : (q + 1) * N]
                out.append(jnp.where(use, new, carried[q]))
            return tuple(out)

        return lax.fori_loop(0, count, one, carried)

    zero = (jnp.zeros((N, LANES), F32),) * 4
    from_below = fold(True, zero)
    from_above = fold(False, zero)
    order = list(range(CHUNKS))
    for q in range(4):
        for value, member, js in (
            (from_below[q], UP_MEMBERS[q], order),
            (from_above[q], DOWN_MEMBERS[q], order[::-1]),
        ):
            target, source = (enter, chunk_h) if q < 2 else (adjoint, chunk_w)
            for j in js:
                rows = pl.ds(j, N, stride=CHUNKS)
                target[member, rows] = value
                value = chunk_p[member, rows] * value + source[member, rows]

    def sweep(member, flipped):
        strand, course = member // 2, lax.rem(member, 2)
        states[: N * CHUNKS] = enter[member]

        def ahead(i, carry):
            hs = list(carry)
            kept = []
            for sub in range(2):
                k = 2 * i + sub
                t = steps - 1 - k if flipped else k
                rows = pl.ds(pl.multiple_of(t * CHUNKS, CHUNKS), CHUNKS)
                s, d, y = step[member, rows], drive[member, rows], dys[strand, rows]
                total = jnp.zeros((CHUNKS, LANES), F32)
                products = []
                for n in range(N):
                    hs[n] = hs[n] * jnp.exp2(s * table[2 + course, n]) + wide[member, rows, columns(n)] * d
                    total = total + wide[member, rows, columns(N + n)] * hs[n]
                    products.append(y * hs[n])
                    at = pl.multiple_of(((k + 1) * N + n) * CHUNKS, CHUNKS)
                    states[pl.ds(at, CHUNKS)] = hs[n]
                out_y[member, rows] = total
                kept.append(products)
            pair = steps // 2 - 1 - i if flipped else i
            rows = pl.ds(pl.multiple_of(pair * 16, 16), 16)
            first, second = (kept[1], kept[0]) if flipped else (kept[0], kept[1])
            for n in range(N):
                both = low(jnp.concatenate([first[n], second[n]], axis=0))
                quads[rows, (N + n) * LANES : (N + n + 1) * LANES] = both
            return tuple(hs)

        start = tuple(enter[member, n * CHUNKS : (n + 1) * CHUNKS] for n in range(N))
        lax.fori_loop(0, steps // 2, ahead, start)

        def back(i, carry):
            cs, ds = list(carry[0]), list(carry[1])
            kept = []
            for sub in range(2):
                k = steps - 1 - (2 * i + sub)
                t = steps - 1 - k if flipped else k
                rows = pl.ds(pl.multiple_of(t * CHUNKS, CHUNKS), CHUNKS)
                s, d, y = step[member, rows], drive[member, rows], dys[strand, rows]
                pulled = jnp.zeros((CHUNKS, LANES), F32)
                slope = jnp.zeros((CHUNKS, LANES), F32)
                products = []
                for n in range(N):
                    lam = y * wide[member, rows, columns(N + n)] + cs[n]
                    pulled = pulled + lam * wide[member, rows, columns(n)]
                    products.append(lam * d)
                    cs[n] = lam * jnp.exp2(s * table[2 + course, n])
                    at = pl.multiple_of((k * N + n) * CHUNKS, CHUNKS)
                    u = cs[n] * states[pl.ds(at, CHUNKS)]
                    slope = slope + u * table[course, n]
                    ds[n] = ds[n] + u * s
                slope_y[member, rows] = slope
                pull_y[member, rows] = pulled
                kept.append(products)
            pair = i if flipped else steps // 2 - 1 - i
            rows = pl.ds(pl.multiple_of(pair * 16, 16), 16)
            first, second = (kept[0], kept[1]) if flipped else (kept[1], kept[0])
            for n in range(N):
                both = low(jnp.concatenate([first[n], second[n]], axis=0))
                quads[rows, n * LANES : (n + 1) * LANES] = both
            return tuple(cs), tuple(ds)

        start = tuple(adjoint[member, n * CHUNKS : (n + 1) * CHUNKS] for n in range(N))
        zeros = (jnp.zeros((CHUNKS, LANES), F32),) * N
        _, ds = lax.fori_loop(0, steps // 2, back, (start, zeros))
        for n in range(N):
            rows = slice(n * CHUNKS, (n + 1) * CHUNKS)
            dacc[course, rows] = dacc[course, rows] + ds[n]
        dproj[member] = nt(spread[:64], quads[...])

    lax.fori_loop(0, 2, lambda i, c: (sweep(3 * i, False), c)[1], 0)
    lax.fori_loop(0, 2, lambda i, c: (sweep(1 + i, True), c)[1], 0)

    small[...] = jnp.zeros_like(small)
    for course in range(2):
        for n in range(N):
            total = jnp.sum(dacc[course, n * CHUNKS : (n + 1) * CHUNKS], axis=0, keepdims=True)
            at = 2 * R + course * N + n
            small[at : at + 1] = total * table[course, n, :1]
    for strand in range(2):
        joined = jnp.zeros((tok, LANES), F32)
        grad = dys[strand]
        for course in range(2):
            member = 2 * strand + course
            active = act[member].astype(F32)
            joined = joined + out_y[member] + tiny[12 + course : 13 + course] * active
            raw_grad = slope_y[member] + pull_y[member] * active
            rounded = low(raw_grad * valid[...] * sigmoid(raw[member]))
            dact[member] = pull_y[member] * step[member] + grad * tiny[12 + course : 13 + course]
            rows = slice(course * R, (course + 1) * R)
            small[rows] += tn(proj[member], rounded)[:R]
            at = 2 * R + 2 * N + course
            small[at : at + 1] += jnp.sum(rounded.astype(F32), axis=0, keepdims=True)
            small[at + 2 : at + 3] += jnp.sum(grad * active, axis=0, keepdims=True)
            message[strand, 64 * course : 64 * course + R] = low(nt(stw[course], rounded))
            message[strand, 64 * course + R : 64 * course + 64] = low(dproj[member, R:])
        gate = gates[strand]
        mixed[strand] = low(joined * silu(gate) * valid[...])
        dgate[strand] = low(gm[strand] * joined * silu_slope(gate))


E_ROWS = 608
L_ROWS = 384
GAIN_ROWS = 16


def halves(pack, total, keep, send):
    half = total // 2
    mine = lax.rem(lax.axis_index("rows"), 2)
    if keep.shape[0] >= total:
        keep[:total] = pack[:total]
        send[:half] = jnp.zeros((half, LANES), BF16)
    else:
        keep[:half] = pack[pl.ds(pl.multiple_of(mine * half, 16), half)]
        send[:half] = low(pack[pl.ds(pl.multiple_of((1 - mine) * half, 16), half)])


def dense_kernel(
    geo, mixed, outs, moved, dgate, normed, weights, back, small, kept, sent, keep, send, g_gate, dn_gate, pack
):
    width = weights.shape[1]
    second = lax.axis_index("ch") >= 2
    branches = []
    grad_out = jnp.zeros((LANES, width), F32)
    grad_gate = jnp.zeros(g_gate.shape, F32)
    for strand in range(2):
        branches.append(nn(low(nn(back[...], mixed[strand])), outs[strand]))
        grad_out = grad_out + tn(mixed[strand], moved[strand])
        grad_gate = grad_gate + tn(normed[strand], dgate[strand])
        dn_gate[strand] = nt(low(nn(back[...], dgate[strand])), weights[1 + 2 * strand])
    kept[...] = jnp.where(second, branches[1], branches[0])
    sent[...] = low(jnp.where(second, branches[0], branches[1]))
    g_gate[...] = grad_gate
    pack[:width] = grad_gate
    pack[width : width + LANES] = grad_out[:, :LANES]
    pack[width + LANES : width + 2 * LANES] = grad_out[:, LANES:]
    pack[width + 2 * LANES : width + 2 * LANES + 80] = small[...]
    pack[width + 2 * LANES + 80 :] = jnp.zeros((16, LANES), F32)
    halves(pack, E_ROWS, keep, send)


def conv_back_kernel(
    geo, one, two, act, dact, pre, padded, tiny, select, normed, rims_normed, gains, w, g_gate, valid, edge,
    res_kept, res_got,
    xg, near, far, keep, send, res_own, res_sent,
    pad_grad, pack,
):
    tok, steps = geo.tok, geo.steps
    taps = (padded.shape[1] // CHUNKS - steps) // 2 + 1
    width = w.shape[1]
    even = lax.rem(lax.axis_index("rows"), 2) == 0
    rim = taps - 1
    sub = iota((CHUNKS, LANES), 0)
    pack[...] = jnp.zeros_like(pack)
    grad_select = [jnp.zeros((64, LANES), F32)] * 2
    grad_in = jnp.zeros((width, LANES), F32)
    at_conv = width + LANES - 32
    for strand in range(2):
        pad_grad[...] = jnp.zeros_like(pad_grad)
        rounded = low(one[strand].astype(F32) + two[strand].astype(F32))
        for course in range(2):
            member = 2 * strand + course
            mine = slice(64 * course, 64 * course + 64)
            grad_select[course] = grad_select[course] + nn(rounded[mine], act[member])
            total = dact[member] + tn(rounded, select[course])
            grad = total * silu_slope(pre[member])
            row = at_conv + 8 + course
            pack[row : row + 1] += jnp.sum(grad, axis=0, keepdims=True)
            for tap in range(taps):
                at = tap_start(tap, taps, FLIPS[member])
                row = at_conv + course * taps + tap
                pack[row : row + 1] += jnp.sum(grad * padded[strand, at : at + tok], axis=0, keepdims=True)
                at_tap = course * taps + tap
                pad_grad[at : at + tok] += tiny[at_tap : at_tap + 1] * grad
        before = [jnp.zeros((1, LANES), F32)] * (16 - rim)
        after = []
        for k in range(rim, 0, -1):
            block = pad_grad[(rim - k) * CHUNKS : (rim - k + 1) * CHUNKS]
            before.append(block[:1])
            moved = jnp.where(sub == CHUNKS - 1, 0.0, pltpu.roll(block, CHUNKS - 1, 0))
            at = (rim + steps - k) * CHUNKS
            pad_grad[at : at + CHUNKS] += moved
        for k in range(rim):
            at = (rim + steps + k) * CHUNKS
            block = pad_grad[at : at + CHUNKS]
            after.append(block[CHUNKS - 1 :])
            moved = jnp.where(sub == 0, 0.0, pltpu.roll(block, 1, 0))
            at = (rim + k) * CHUNKS
            pad_grad[at : at + CHUNKS] += moved
        after += [jnp.zeros((1, LANES), F32)] * (16 - rim)
        rims = jnp.concatenate(before + after, axis=0) * edge[...]
        main = pad_grad[rim * CHUNKS : (rim + steps) * CHUNKS]
        xg[strand] = main
        grad_in = grad_in + tn(normed[strand], low(main * valid[...])) + tn(rims_normed[strand], low(rims))
        near[strand] = jnp.where(even, rims[16:], rims[:16])
        far[strand] = jnp.where(even, rims[:16], rims[16:])
    pack[:width] = grad_in
    amount = LANES // 2 - 16
    for course in range(2):
        pack[width + course * amount : width + (course + 1) * amount] = grad_select[course][:amount]
    halves(pack, L_ROWS, keep, send)
    product = grad_in * w[0].astype(F32) + g_gate[...] * w[1].astype(F32)
    high = low(product)
    ones = jnp.ones((8, LANES), BF16)
    gain_part = (nt(ones, high) + nt(ones, low(product - high.astype(F32)))) / gains[:1]
    at = keep.shape[0] - GAIN_ROWS
    keep[at : at + 8] = gain_part[:, :LANES]
    keep[at + 8 :] = gain_part[:, LANES:]
    at = send.shape[0] - GAIN_ROWS
    send[at:] = low(jnp.concatenate([gain_part[:, :LANES], gain_part[:, LANES:]], axis=0))
    total = res_kept[...] + res_got[...].astype(F32)
    odd = lax.rem(lax.axis_index("ch"), 2) == 1
    res_own[...] = jnp.where(odd, total[:, LANES:], total[:, :LANES])
    res_sent[...] = low(jnp.where(odd, total[:, :LANES], total[:, LANES:]))


def normed_back_kernel(
    geo, xg, near, far, dn_gate, weights, valid, back, hidden, res_own, res_got, kept, sent, result
):
    tok, steps = geo.tok, geo.steps
    even = lax.rem(lax.axis_index("rows"), 2) == 0
    second = lax.axis_index("ch") >= 2
    row = iota((tok, LANES), 0)
    token = (row % CHUNKS) * steps + row // CHUNKS
    grads = []
    for strand in range(2):
        one, two = near[strand], far[strand]
        ahead = jnp.where(even, two, one)
        behind = jnp.where(even, one, two)
        total = xg[strand]
        for k in range(3):
            total = total + jnp.where(token == k, ahead[k : k + 1], 0.0)
            total = total + jnp.where(token == tok - 1 - k, behind[15 - k : 16 - k], 0.0)
        rounded = low(total * valid[...])
        grads.append(nt(low(nn(back[...], rounded)), weights[2 * strand]) + dn_gate[strand])
    kept[...] = jnp.where(second, grads[1], grads[0])
    sent[...] = low(jnp.where(second, grads[0], grads[1]))
    out = hidden[...].astype(F32) + res_own[...] + res_got[...].astype(F32)
    result[...] = low(out)


def finish_kernel(geo, one, two, xo, xc, gains, cot, input_grad):
    mine = lax.axis_index("ch")
    odd = lax.rem(mine, 2) == 1
    a, b = xo[...].astype(F32), xc[...].astype(F32)
    source = jnp.concatenate([jnp.where(odd, b, a), jnp.where(odd, a, b)], axis=1)
    inverse = lax.rsqrt(jnp.mean(source * source, axis=-1, keepdims=True) + EPSILON)
    unit = source * inverse
    here = jnp.where(mine >= 2, gains[1:], gains[:1])
    scaled = (one[...].astype(F32) + two[...].astype(F32)) * here
    back = inverse * (scaled - unit * jnp.mean(scaled * unit, axis=-1, keepdims=True))
    input_grad[...] = cot[...].astype(F32) + jnp.where(odd, back[:, LANES:], back[:, :LANES])


def unpack_kernel(e_parts, l_parts, gain_sum, in_g, out_g, sel_g, cw_g, cb_g, stw_g, stb_g, decay_g, skip_g, gain_g, e_pack, l_pack):
    mine = lax.rem(lax.axis_index("rows"), 2)
    for parts, pack in ((e_parts, e_pack), (l_parts, l_pack)):
        total = pack.shape[0]
        half = total // 2
        if len(parts) == 1:
            pack[...] = parts[0][:total].astype(F32)
        else:
            pack[pl.ds(pl.multiple_of(mine * half, 16), half)] = parts[0][:half].astype(F32)
            pack[pl.ds(pl.multiple_of((1 - mine) * half, 16), half)] = parts[1][:half].astype(F32)
    width = in_g.shape[1]
    in_g[0] = l_pack[:width]
    in_g[1] = e_pack[:width]
    out_g[:, :LANES] = e_pack[width : width + LANES]
    out_g[:, LANES:] = e_pack[width + LANES : width + 2 * LANES]
    amount = sel_g.shape[1]
    for course in range(2):
        sel_g[course] = l_pack[width + course * amount : width + (course + 1) * amount]
    at = width + 2 * amount
    taps = cw_g.shape[1]
    for course in range(2):
        cw_g[course] = l_pack[at + course * taps : at + (course + 1) * taps]
    cb_g[...] = l_pack[at + 2 * taps : at + 2 * taps + 2]
    at = width + 2 * LANES
    for course in range(2):
        stw_g[course] = e_pack[at + course * R : at + (course + 1) * R]
        decay_g[course] = e_pack[at + 2 * R + course * N : at + 2 * R + (course + 1) * N]
    at = at + 2 * R + 2 * N
    stb_g[...] = e_pack[at : at + 2]
    skip_g[...] = e_pack[at + 2 : at + 4]
    gain_g[:, :LANES] = gain_sum[:1].astype(F32)
    gain_g[:, LANES:] = gain_sum[8:9].astype(F32)


def swap(value, axis, distance):
    count = lax.axis_size(axis)
    return lax.ppermute(value, axis, [(i, i ^ distance) for i in range(count)])


def gather_channels(value):
    across = swap(value, "ch", 2)
    return value, swap(value, "ch", 1), across, swap(across, "ch", 1)


def partner_sum(value):
    joined = low(value.astype(F32) + swap(value, "ch", 2).astype(F32))
    return joined, swap(joined, "ch", 1)


def on_device(
    hidden_in, lengths, norm_gain, in_weight, conv_weight, conv_bias, select_weight,
    step_weight, step_bias, decay_log, skip_gain, out_weight, cotangent,
):
    tok = hidden_in.shape[0]
    rows = lax.axis_size("rows")
    geo = Geometry(tok, rows)
    steps = geo.steps
    width = in_weight.shape[1]
    gain = norm_gain[None, :]
    small_mesh = geo.members == 4 and rows == 8
    padded_rows = (steps + 2 * (conv_weight.shape[1] - 1)) * CHUNKS

    def kernel(f):
        return functools.partial(f, geo)

    def lifted(f, first, amount):
        def body(*refs):
            return f(*refs[:first], refs[first : first + amount], *refs[first + amount :])

        return body

    vm = pltpu.VMEM
    strands = ((2, tok, LANES), F32)
    strands_low = ((2, tok, LANES), BF16)
    members = ((4, tok, LANES), F32)
    members_low = ((4, tok, LANES), BF16)
    chunked = ((4, N * CHUNKS, LANES), F32)
    summary = ((4 * N + 8, LANES), F32)
    full = ((tok, width), F32)
    full_low = ((tok, width), BF16)

    x_parts = gather_channels(hidden_in)
    x_own, c_own, valid, edge, turn, mover, back, gains, weights, outs, select, table, spread, tiny, stw = run(
        kernel(prepare_kernel),
        [
            ((tok, LANES), BF16),
            ((tok, LANES), BF16),
            ((tok, LANES), F32),
            ((32, LANES), F32),
            ((width, width), BF16),
            ((tok, tok), BF16),
            ((tok, tok), BF16),
            ((2, width), F32),
            ((4, width, LANES), BF16),
            ((2, LANES, width), BF16),
            ((2, LANES, LANES), BF16),
            ((4, N, CHUNKS, LANES), F32),
            ((LANES, 2 * N * LANES), BF16),
            ((24 + 2 * N, LANES), F32),
            (step_weight.shape, BF16),
        ],
        lengths, hidden_in, cotangent, in_weight, out_weight, step_weight, gain, conv_weight, conv_bias,
        jnp.swapaxes(select_weight, 1, 2), step_bias, decay_log, skip_gain,
        anywhere=13,
        scratch=[
            pltpu.SMEM(lengths.shape, jnp.int32),
            vm(gain.shape, F32),
            vm(conv_weight.shape, F32),
            vm(conv_bias.shape, F32),
            vm((2, select_weight.shape[2], LANES), BF16),
            vm(step_bias.shape, F32),
            vm(decay_log.shape, F32),
            vm(skip_gain.shape, F32),
            pltpu.SemaphoreType.DMA((13,)),
        ],
        micros=2,
    )
    x_parts = (x_own,) + x_parts[1:]
    c_parts = (c_own,) + gather_channels(cotangent)[1:]

    normed, inputs, gates, near, far = run(
        kernel(project_kernel),
        [((2, tok, width), BF16), strands_low, strands, ((16, 2 * width), BF16), ((16, 2 * width), BF16)],
        *x_parts, valid, turn, mover, gains, weights,
        scratch=[vm((4, tok, LANES), BF16)],
    )
    near = lax.ppermute(near, "rows", geo.near())
    far = lax.ppermute(far, "rows", geo.far())
    moved, gm, dys = run(
        kernel(cotangent_kernel),
        [((2, tok, width), BF16), strands, strands],
        *c_parts, gates, valid, turn, mover, outs,
        scratch=[vm((4, tok, LANES), BF16)], micros=1,
    )
    padded, rims_normed, pre, act, message = run(
        kernel(conv_kernel),
        [((2, padded_rows, LANES), F32), ((2, 32, width), BF16), members, members_low, strands_low],
        inputs, near, far, edge, turn, gains, weights, select, tiny, dys,
    )
    one, two = partner_sum(message)
    shapes = [members_low, members, members, members, chunked, chunked, chunked]
    shapes += [((4, tok, 2 * N * LANES), F32)]

    def summarise(*refs):
        if small_mesh:
            summary_kernel(geo, *refs)
        else:
            summary_kernel(geo, *refs[:17], None, None, *refs[17:])

    got = run(
        summarise, shapes + [summary, summary],
        one, two, act, dys, stw, tiny, table, spread, valid,
        scratch=[vm(summary[0], F32), vm(summary[0], F32)] if small_mesh else (), micros=10,
    )
    proj, raw, step, drive, chunk_p, chunk_h, chunk_w, wide = got[:8]
    if small_mesh:
        slots = (
            lax.ppermute(got[8], "rows", geo.near()),
            lax.ppermute(got[9], "rows", geo.across()),
            lax.ppermute(got[9], "rows", geo.far()),
        )
        slot_scratch = vm((4,) + summary[0], F32)
    else:
        up, down = lax.all_gather(got[8], "rows"), lax.all_gather(got[9], "rows")
        place = lax.axis_index("rows")
        index = place - geo.local() + jnp.arange(geo.members)
        inside = jnp.clip(index, 0, rows - 1)
        slots = (jnp.where((index < place)[:, None, None], up[inside], down[inside]),)
        slot_scratch = vm((8, LANES), F32)
    mixed, dgate, dact, message, small = run(
        lifted(kernel(scan_kernel), 0, len(slots)),
        [strands_low, strands_low, members, ((2, LANES, tok), BF16), ((80, LANES), F32)],
        *slots, act, proj, raw, step, drive, chunk_p, chunk_h, chunk_w, wide, spread,
        dys, gm, gates, stw, tiny, table, valid,
        scratch=[
            slot_scratch,
            vm(chunked[0], F32),
            vm(chunked[0], F32),
            vm(((steps + 1) * N * CHUNKS, LANES), F32),
            vm((tok, 2 * N * LANES), BF16),
            vm(members[0], F32),
            vm(members[0], F32),
            vm(members[0], F32),
            vm((4, 64, tok), F32),
            vm((2, N * CHUNKS, LANES), F32),
        ],
        micros=16, limit=14,
    )
    one, two = partner_sum(message)
    e_half = E_ROWS // 2
    l_half = L_ROWS // 2 + GAIN_ROWS
    res_kept, res_sent, e_keep, e_send, g_gate, dn_gate = run(
        kernel(dense_kernel),
        [
            full,
            full_low,
            ((e_half if small_mesh else E_ROWS, LANES), F32),
            ((e_half, LANES), BF16),
            ((width, LANES), F32),
            ((2, tok, width), F32),
        ],
        mixed, outs, moved, dgate, normed, weights, back, small,
        scratch=[vm((E_ROWS, LANES), F32)],
    )
    res_got = swap(res_sent, "ch", 2)
    if small_mesh:
        e_sum = low(e_keep + swap(e_send, "rows", 1).astype(F32))
    xg, near, far, l_keep, l_send, res_own, res_sent = run(
        kernel(conv_back_kernel),
        [
            strands,
            ((2, 16, LANES), F32),
            ((2, 16, LANES), F32),
            ((l_half if small_mesh else L_ROWS + GAIN_ROWS, LANES), F32),
            ((l_half, LANES), BF16),
            ((tok, LANES), F32),
            ((tok, LANES), BF16),
        ],
        one, two, act, dact, pre, padded, tiny, select, normed, rims_normed, gains, weights, g_gate, valid, edge,
        res_kept, res_got,
        scratch=[vm((padded_rows, LANES), F32), vm((L_ROWS, LANES), F32)],
    )
    near = lax.ppermute(near, "rows", geo.near())
    if small_mesh:
        l_sum = low(l_keep + swap(l_send, "rows", 1).astype(F32))
        e_sum = low(e_sum.astype(F32) + swap(e_sum, "rows", 2).astype(F32))
    far = lax.ppermute(far, "rows", geo.far())
    res_got = swap(res_sent, "ch", 1)
    dn_kept, dn_sent, result = run(
        kernel(normed_back_kernel),
        [full, full_low, ((tok, LANES), BF16)],
        xg, near, far, dn_gate, weights, valid, back, x_own, res_own, res_got,
    )
    dn_got = swap(dn_sent, "ch", 2)
    dn = low(dn_kept + dn_got.astype(F32))
    input_grad = run(
        kernel(finish_kernel), ((tok, LANES), F32),
        dn, swap(dn, "ch", 1), x_parts[0], x_parts[1], gains, c_own,
    )
    if small_mesh:
        l_sum = low(l_sum.astype(F32) + swap(l_sum, "rows", 2).astype(F32))
        e_sum = low(e_sum.astype(F32) + swap(e_sum, "rows", 4).astype(F32))
        l_sum = low(l_sum.astype(F32) + swap(l_sum, "rows", 4).astype(F32))
        e_parts = (e_sum, swap(e_sum, "rows", 1))
        l_parts = (l_sum, swap(l_sum, "rows", 1))
        gain_part = l_sum[l_half - GAIN_ROWS :].astype(F32)
        gain_part = gain_part + swap(gain_part, "ch", 2)
        gain_part = gain_part + swap(gain_part, "ch", 1)
    else:
        e_parts = (lax.psum(e_keep, "rows"),)
        l_parts = (lax.psum(l_keep, "rows"),)
        gain_part = lax.psum(l_parts[0][L_ROWS:], "ch")

    def unpack(*refs):
        k = len(e_parts)
        unpack_kernel(refs[:k], refs[k : 2 * k], *refs[2 * k :])

    got = run(
        unpack,
        [
            (in_weight.shape, F32),
            (out_weight.shape, F32),
            (jnp.swapaxes(select_weight, 1, 2).shape, F32),
            (conv_weight.shape, F32),
            (conv_bias.shape, F32),
            (step_weight.shape, F32),
            (step_bias.shape, F32),
            (decay_log.shape, F32),
            (skip_gain.shape, F32),
            ((1, width), F32),
        ],
        *e_parts, *l_parts, gain_part,
        scratch=[vm((E_ROWS, LANES), F32), vm((L_ROWS, LANES), F32)],
    )
    in_g, out_g, sel_g, cw_g, cb_g, stw_g, stb_g, decay_g, skip_g, gain_g = got
    return (
        result, input_grad, gain_g[0], in_g, cw_g, cb_g, jnp.swapaxes(sel_g, 1, 2), stw_g, stb_g, decay_g, skip_g, out_g,
    )


def solution(mesh):
    lanes = P(None, None, "ch")
    pair = P(None, "ch")
    columns = P(None, "ch", None)
    tokens = P("rows", "ch")
    return jax.shard_map(
        on_device,
        mesh=mesh,
        in_specs=(
            tokens, P(), P(), lanes, lanes, pair, columns, lanes, pair, lanes, pair, P("ch", None), tokens,
        ),
        out_specs=(
            tokens, tokens, P(), lanes, lanes, pair, columns, lanes, pair, lanes, pair, P("ch", None),
        ),
        check_vma=False,
    )
```

```python
import functools

import jax
import jax.numpy as jnp
from jax import lax
from jax.experimental import pallas as pl
from jax.experimental.pallas import tpu as pltpu
from jax.sharding import PartitionSpec as P


N = 16
R = 16
WINDOW = 16384
LANES = 128
CHUNKS = 8
COLUMNS = R + 2 * N
EPSILON = 1e-06
LOG2E = 1.4426950408889634
F32 = jnp.float32
BF16 = jnp.bfloat16
VM = pl.BlockSpec(memory_space=pltpu.VMEM)
FLIPS = (False, True, True, False)


def nn(left, right):
    return lax.dot_general(left, right, (((1,), (0,)), ((), ())), preferred_element_type=F32)


def nt(left, right):
    return lax.dot_general(left, right, (((1,), (1,)), ((), ())), preferred_element_type=F32)


def tn(left, right):
    return lax.dot_general(left, right, (((0,), (0,)), ((), ())), preferred_element_type=F32)


def iota(shape, dim):
    return lax.broadcasted_iota(jnp.int32, shape, dim)


def one_hot(mask):
    return jnp.where(mask, 1.0, 0.0).astype(BF16)


def permuter(tok):
    steps = tok // CHUNKS
    row, col = iota((tok, tok), 0), iota((tok, tok), 1)
    return one_hot((row % CHUNKS) * steps + row // CHUNKS == col)


def unpermuter(tok):
    steps = tok // CHUNKS
    row, col = iota((tok, tok), 0), iota((tok, tok), 1)
    return one_hot((col % CHUNKS) * steps + col // CHUNKS == row)


def mirror(width):
    return one_hot(iota((width, width), 0) + iota((width, width), 1) == width - 1)


def sigmoid(v):
    return 1.0 / (1.0 + jnp.exp(-v))


def silu(v):
    return v * sigmoid(v)


def silu_slope(v):
    logistic = sigmoid(v)
    return logistic * (1.0 + v * (1.0 - logistic))


def softplus(v):
    return jnp.maximum(v, 0.0) + jnp.log1p(jnp.exp(-jnp.abs(v)))


def low(v):
    return v.astype(BF16)


class Geometry:
    def __init__(self, tok, rows):
        self.tok = tok
        self.rows = rows
        self.window = min(WINDOW, tok * rows // 2)
        self.members = self.window // tok
        self.steps = tok // CHUNKS

    def place(self, lengths_ref):
        row = lax.axis_index("rows")
        shifted = row * self.tok + self.window // 2
        offset = lax.rem(shifted, self.window)
        length = lengths_ref[lax.div(shifted, self.window)]
        return row, offset, length

    def valid(self, lengths_ref):
        _, offset, length = self.place(lengths_ref)
        row = iota((self.tok, 1), 0)
        token = (row % CHUNKS) * self.steps + row // CHUNKS
        return jnp.where(offset + token < length, 1.0, 0.0)

    def local(self):
        row = lax.axis_index("rows")
        return lax.rem(row + self.members // 2, self.members)

    def near(self):
        return [(i, i ^ 1) for i in range(self.rows)]

    def far(self):
        if self.members == 4:
            return self.swaps(lambda k: 3 - k)
        out = []
        for i in range(1, self.rows, 2):
            out += [(i, (i + 1) % self.rows), ((i + 1) % self.rows, i)]
        return out

    def across(self):
        return self.swaps(lambda k: (k + 2) % 4)

    def swaps(self, other):
        out = []
        for i in range(self.rows):
            local = (i + 2) % 4
            j = i - local + other(local)
            out.append((i, j if 0 <= j < self.rows else i ^ 1))
        return out


def run(kernel, outs, *args, anywhere=0, scratch=(), micros=1, limit=8):
    single = isinstance(outs, tuple)
    shapes = [outs] if single else list(outs)
    args = [pltpu.with_memory_space_constraint(a, pltpu.HBM) for a in args[:anywhere]] + list(args[anywhere:])
    call = pl.pallas_call(
        kernel,
        out_shape=[jax.ShapeDtypeStruct(s, d) for s, d in shapes],
        in_specs=[pl.BlockSpec(memory_space=pltpu.HBM)] * anywhere + [VM] * (len(args) - anywhere),
        out_specs=[VM] * len(shapes),
        scratch_shapes=list(scratch),
        compiler_params=pltpu.CompilerParams(vmem_limit_bytes=limit * 1024 * 1024),
        cost_estimate=pl.CostEstimate(flops=0, bytes_accessed=int(micros * 3.0e6), transcendentals=0),
    )
    got = call(*args)
    return got[0] if single else got


def assemble(refs, scratch):
    mine = lax.axis_index("ch")
    for distance, ref in enumerate(refs):
        scratch[lax.bitwise_xor(mine, distance)] = ref[...]
    return (
        jnp.concatenate([scratch[0], scratch[1]], axis=1),
        jnp.concatenate([scratch[2], scratch[3]], axis=1),
    )


def prepare_kernel(
    geo, lengths_in, x_in, c_in, w_in, ow_in, stw_in, gain_in, cw_in, cb_in, sw_in, stb_in, decay_in, skip_in,
    x_out, c_out, valid, edge, turn, mover, back, gains, weights, outs, select, table, spread, tiny, stw,
    lengths, gain, cw, cb, stb, decay, skip, sems,
):
    pairs = (
        (lengths_in, lengths), (w_in, weights.at[0:2]), (ow_in, outs.at[0]), (stw_in, stw), (gain_in, gain),
        (cw_in, cw), (cb_in, cb), (sw_in, select), (stb_in, stb), (decay_in, decay), (skip_in, skip),
        (x_in, x_out), (c_in, c_out),
    )
    copies = [pltpu.make_async_copy(source, target, sems.at[i]) for i, (source, target) in enumerate(pairs)]
    for copy in copies:
        copy.start()
    tok = geo.tok
    width = turn.shape[0]
    flip = mirror(width)
    turn[...] = flip
    mover[...] = permuter(tok)
    back[...] = unpermuter(tok)
    for at in range(0, 2 * N):
        key = iota((2 * COLUMNS, LANES), 0) % COLUMNS
        spread[:, at * LANES : (at + 1) * LANES] = one_hot(key == R + at)
    tiny[...] = jnp.zeros_like(tiny)
    for copy in copies:
        copy.wait()
    valid[...] = jnp.broadcast_to(geo.valid(lengths), valid.shape)
    edge[...] = jnp.broadcast_to(rim_valid(geo, lengths), edge.shape)
    plain = jnp.broadcast_to(gain[...], (8, width))
    high = low(plain)
    rest = plain - high.astype(F32)
    middle = low(rest)
    turned = nn(high, flip) + nn(middle, flip) + nn(low(rest - middle.astype(F32)), flip)
    gains[:1] = gain[...]
    gains[1:] = turned[:1]
    for k in range(2):
        weights[2 + k] = low(nn(flip, weights[k]))
    outs[1] = low(nn(outs[0], flip))
    for course in range(2):
        natural = -jnp.exp(decay[course])
        for n in range(N):
            level = jnp.broadcast_to(natural[n : n + 1], (CHUNKS, LANES))
            table[course, n] = level
            table[2 + course, n] = level * LOG2E
    taps = cw.shape[1]
    for course in range(2):
        tiny[course * taps : (course + 1) * taps] = cw[course]
        tiny[24 + course * N : 24 + (course + 1) * N] = -LOG2E * jnp.exp(decay[course])
    tiny[8:10] = cb[...]
    tiny[10:12] = stb[...]
    tiny[12:14] = skip[...]


def project_kernel(geo, xo, xc, xy, xd, valid, turn, mover, gains, w, normed, inputs, gates, near, far, scratch):
    tok = geo.tok
    width = w.shape[1]
    sides = assemble((xo, xc, xy, xd), scratch)
    even = lax.rem(lax.axis_index("rows"), 2) == 0
    for half, side in enumerate(sides):
        first, last = side[:16], side[tok - 16 :]
        lanes = slice(half * width, (half + 1) * width)
        near[:, lanes] = jnp.where(even, last.astype(F32), first.astype(F32)).astype(BF16)
        far[:, lanes] = jnp.where(even, first.astype(F32), last.astype(F32)).astype(BF16)
    both = jnp.concatenate([w[0], w[1]], axis=1)
    for strand in range(2):
        side = sides[strand]
        if strand == 1:
            side = low(nn(side, turn[...]))
        source = nn(mover[...], side)
        inverse = lax.rsqrt(jnp.mean(source * source, axis=-1, keepdims=True) + EPSILON)
        rows = low(source * inverse * gains[:1])
        normed[strand] = rows
        out = nn(rows, both)
        lanes = out.shape[1] // 2
        inputs[strand] = low(out[:, :lanes] * valid[...])
        gates[strand] = out[:, lanes:]


def cotangent_kernel(geo, co, cc, cy, cd, gates, valid, turn, mover, outs, moved, gm, dys, scratch):
    sides = assemble((co, cc, cy, cd), scratch)
    for strand in range(2):
        side = sides[strand]
        if strand == 1:
            side = low(nn(side, turn[...]))
        rows = low(nn(mover[...], side))
        moved[strand] = rows
        grad = nt(rows, outs[0]) * valid[...]
        gm[strand] = grad
        dys[strand] = grad * silu(gates[strand])


def rim_valid(geo, lengths_ref):
    _, offset, length = geo.place(lengths_ref)
    row = iota((32, 1), 0)
    token = jnp.where(row < 16, row - 16, geo.tok + row - 16) + offset
    index = token - offset + lax.axis_index("rows") * geo.tok
    inside = (token >= 0) & (token < geo.window) & (token < length)
    inside = inside & (index >= 0) & (index < geo.tok * geo.rows)
    return jnp.where(inside, 1.0, 0.0)


def fill_padded(padded, main, rims, steps):
    rim = padded.shape[0] // CHUNKS - steps
    rim = rim // 2
    lanes = main.shape[1]
    sub = iota((CHUNKS, lanes), 0)
    padded[rim * CHUNKS : (rim + steps) * CHUNKS] = main
    for k in range(1, rim + 1):
        block = main[(steps - k) * CHUNKS : (steps - k + 1) * CHUNKS]
        moved = pltpu.roll(block, 1, 0)
        edge = jnp.broadcast_to(rims[16 - k : 17 - k], (CHUNKS, lanes))
        padded[(rim - k) * CHUNKS : (rim - k + 1) * CHUNKS] = jnp.where(sub == 0, edge, moved)
    for k in range(rim):
        block = main[k * CHUNKS : (k + 1) * CHUNKS]
        moved = pltpu.roll(block, CHUNKS - 1, 0)
        edge = jnp.broadcast_to(rims[16 + k : 17 + k], (CHUNKS, lanes))
        at = rim + steps + k
        padded[at * CHUNKS : (at + 1) * CHUNKS] = jnp.where(sub == CHUNKS - 1, edge, moved)


def tap_start(tap, taps, flipped):
    return (2 * (taps - 1) - tap if flipped else tap) * CHUNKS


def conv_kernel(
    geo, inputs, near, far, edge, turn, gains, w, select, tiny, after, padded, rims_normed, pre, act, message
):
    tok, steps = geo.tok, geo.steps
    taps = (padded.shape[1] // CHUNKS - steps) // 2 + 1
    lanes = w.shape[2]
    width = w.shape[1]
    even = lax.rem(lax.axis_index("rows"), 2) == 0
    for strand in range(2):
        part = slice(strand * width, (strand + 1) * width)
        one, two = near[:, part].astype(F32), far[:, part].astype(F32)
        source = jnp.concatenate([jnp.where(even, two, one), jnp.where(even, one, two)], axis=0)
        if strand == 1:
            source = nn(low(source), turn[...])
        inverse = lax.rsqrt(jnp.mean(source * source, axis=-1, keepdims=True) + EPSILON)
        rows = low(source * inverse * gains[:1])
        rims_normed[strand] = rows
        edges = low(nn(rows, w[0]) * edge[...]).astype(F32)
        main = inputs[strand].astype(F32)
        fill_padded(padded.at[strand], main, edges, steps)
        for course in range(2):
            member = 2 * strand + course
            running = jnp.broadcast_to(tiny[8 + course : 9 + course], (tok, lanes))
            for tap in range(taps):
                at = tap_start(tap, taps, FLIPS[member])
                row = course * taps + tap
                running = running + tiny[row : row + 1] * padded[strand, at : at + tok]
            pre[member] = running
            active = low(silu(running))
            act[member] = active
            message[strand, COLUMNS * course : COLUMNS * (course + 1)] = low(nt(select[course], active))


def columns(n):
    return slice(n * LANES, (n + 1) * LANES)


def summary_kernel(
    geo, split_devices, one, two, act, dys, stw, tiny, table, spread, valid,
    proj, raw, step, drive, chunk_p, chunk_h, chunk_w, wide, near, far, up, down,
):
    steps = geo.steps
    for strand in range(2):
        total = one[strand].astype(F32) + two[strand].astype(F32)
        for course in range(2):
            member = 2 * strand + course
            here = total[COLUMNS * course : COLUMNS * (course + 1)]
            rounded = low(here)
            proj[member] = rounded
            rest = here - rounded.astype(F32)
            split = low(jnp.concatenate([here, rest], axis=0).T)
            for at in range(0, 2 * N * LANES, 512):
                wide[member, :, at : at + 512] = nn(split, spread[:, at : at + 512])
            step_raw = tn(rounded[:R], stw[course]) + tiny[10 + course : 11 + course]
            step_row = softplus(step_raw) * valid[...]
            raw[member] = step_raw
            step[member] = step_row
            drive[member] = step_row * act[member].astype(F32)

    def sweep(member, flipped):
        strand, course = member // 2, lax.rem(member, 2)
        for base in range(0, N, 8):

            def body(k, carry):
                ps, hs, ws = (list(c) for c in carry)
                t = steps - 1 - k if flipped else k
                rows = pl.ds(pl.multiple_of(t * CHUNKS, CHUNKS), CHUNKS)
                s, d, y = step[member, rows], drive[member, rows], dys[strand, rows]
                for i in range(8):
                    n = base + i
                    decay_here = jnp.exp2(s * table[2 + course, n])
                    ps[i] = ps[i] * decay_here
                    hs[i] = hs[i] * decay_here + wide[member, rows, columns(n)] * d
                    ws[i] = ws[i] + ps[i] * (wide[member, rows, columns(N + n)] * y)
                return tuple(ps), tuple(hs), tuple(ws)

            zero = jnp.zeros((CHUNKS, LANES), F32)
            start = (tuple([zero + 1.0] * 8), (zero,) * 8, (zero,) * 8)
            ps, hs, ws = lax.fori_loop(0, steps, body, start, unroll=4)
            for i in range(8):
                rows = slice((base + i) * CHUNKS, (base + i + 1) * CHUNKS)
                chunk_p[member, rows] = ps[i]
                chunk_h[member, rows] = hs[i]
                chunk_w[member, rows] = ws[i]

    lax.fori_loop(0, 2, lambda i, c: (sweep(3 * i, False), c)[1], 0)
    lax.fori_loop(0, 2, lambda i, c: (sweep(1 + i, True), c)[1], 0)

    slots = {0: (0, 2), 3: (1, 3), 1: (2, 0), 2: (3, 1)}
    for member in range(4):
        h = jnp.zeros((N, LANES), F32)
        w = jnp.zeros((N, LANES), F32)
        order = list(range(CHUNKS))
        forward = order[::-1] if FLIPS[member] else order
        for j in forward:
            rows = pl.ds(j, N, stride=CHUNKS)
            h = chunk_p[member, rows] * h + chunk_h[member, rows]
        for j in forward[::-1]:
            rows = pl.ds(j, N, stride=CHUNKS)
            w = chunk_p[member, rows] * w + chunk_w[member, rows]
        length = jnp.sum(step[member], axis=0, keepdims=True)
        slot_up, slot_down = slots[member]
        goes_up, goes_down = (w, h) if FLIPS[member] else (h, w)
        up[slot_up * N : (slot_up + 1) * N] = goes_up
        down[slot_down * N : (slot_down + 1) * N] = goes_down
        high = low(length).astype(F32)
        for message, slot in ((up, slot_up), (down, slot_down)):
            message[4 * N + slot : 4 * N + slot + 1] = high
            message[4 * N + 4 + slot : 4 * N + 5 + slot] = length - high
    up[4 * N + 8 :] = jnp.zeros((8, LANES), F32)
    down[4 * N + 8 :] = jnp.zeros((8, LANES), F32)
    if split_devices:
        local = geo.local()
        near[...] = low(jnp.where(lax.rem(local, 2) == 0, up[...], down[...]))
        far[...] = low(jnp.where(local < 2, up[...], down[...]))
    else:
        near[...] = low(up[...])
        far[...] = low(down[...])


UP_MEMBERS = (0, 3, 1, 2)
DOWN_MEMBERS = (1, 2, 0, 3)


def scan_kernel(
    geo, slot_refs, act, proj, raw, step, drive, chunk_p, chunk_h, chunk_w, wide, spread,
    dys, gm, gates, stw, tiny, table, valid,
    mixed, dgate, dact, message, small,
    slots, enter, adjoint, states, quads, out_y, slope_y, pull_y, dproj, dacc,
):
    tok, steps = geo.tok, geo.steps
    count = geo.members
    row = lax.axis_index("rows")
    local = geo.local()
    base_row = row - local
    if len(slot_refs) == 1:
        slots = slot_refs[0]
    else:
        slots[local] = jnp.zeros(slots.shape[1:], BF16)
        others = (lax.bitwise_xor(local, 1), lax.rem(local + 2, 4), 3 - local)
        for at, ref in zip(others, slot_refs):
            slots[at] = ref[...]
    dacc[...] = jnp.zeros_like(dacc)

    def fold(ascending, carried):
        members = UP_MEMBERS if ascending else DOWN_MEMBERS
        tables = [tiny[24 + N * (m % 2) : 24 + N * (m % 2) + N] for m in members]

        def one(i, carried):
            k = i if ascending else count - 1 - i
            there = base_row + k
            use = (k < local) if ascending else (k > local)
            use = use & (there >= 0) & (there < geo.rows)
            out = []
            for q in range(4):
                lengths = slots[k, 4 * N : 5 * N].astype(F32)
                length = lengths[q : q + 1] + lengths[4 + q : 5 + q]
                new = jnp.exp2(tables[q] * length) * carried[q] + slots[k, q * N : (q + 1) * N].astype(F32)
                out.append(jnp.where(use, new, carried[q]))
            return tuple(out)

        return lax.fori_loop(0, count, one, carried)

    zero = (jnp.zeros((N, LANES), F32),) * 4
    from_below = fold(True, zero)
    from_above = fold(False, zero)
    order = list(range(CHUNKS))
    for q in range(4):
        for value, member, js in (
            (from_below[q], UP_MEMBERS[q], order),
            (from_above[q], DOWN_MEMBERS[q], order[::-1]),
        ):
            target, source = (enter, chunk_h) if q < 2 else (adjoint, chunk_w)
            for j in js:
                rows = pl.ds(j, N, stride=CHUNKS)
                target[member, rows] = value
                value = chunk_p[member, rows] * value + source[member, rows]

    def sweep(member, flipped):
        strand, course = member // 2, lax.rem(member, 2)
        states[: N * CHUNKS] = enter[member]

        def ahead(i, carry):
            hs = list(carry)
            kept = []
            for sub in range(2):
                k = 2 * i + sub
                t = steps - 1 - k if flipped else k
                rows = pl.ds(pl.multiple_of(t * CHUNKS, CHUNKS), CHUNKS)
                s, d, y = step[member, rows], drive[member, rows], dys[strand, rows]
                total = jnp.zeros((CHUNKS, LANES), F32)
                products = []
                for n in range(N):
                    hs[n] = hs[n] * jnp.exp2(s * table[2 + course, n]) + wide[member, rows, columns(n)] * d
                    total = total + wide[member, rows, columns(N + n)] * hs[n]
                    products.append(y * hs[n])
                    at = pl.multiple_of(((k + 1) * N + n) * CHUNKS, CHUNKS)
                    states[pl.ds(at, CHUNKS)] = hs[n]
                out_y[member, rows] = total
                kept.append(products)
            pair = steps // 2 - 1 - i if flipped else i
            rows = pl.ds(pl.multiple_of(pair * 16, 16), 16)
            first, second = (kept[1], kept[0]) if flipped else (kept[0], kept[1])
            for n in range(N):
                both = low(jnp.concatenate([first[n], second[n]], axis=0))
                quads[rows, (N + n) * LANES : (N + n + 1) * LANES] = both
            return tuple(hs)

        start = tuple(enter[member, n * CHUNKS : (n + 1) * CHUNKS] for n in range(N))
        lax.fori_loop(0, steps // 2, ahead, start)

        def back(i, carry):
            cs, ds = list(carry[0]), list(carry[1])
            kept = []
            for sub in range(2):
                k = steps - 1 - (2 * i + sub)
                t = steps - 1 - k if flipped else k
                rows = pl.ds(pl.multiple_of(t * CHUNKS, CHUNKS), CHUNKS)
                s, d, y = step[member, rows], drive[member, rows], dys[strand, rows]
                pulled = jnp.zeros((CHUNKS, LANES), F32)
                slope = jnp.zeros((CHUNKS, LANES), F32)
                products = []
                for n in range(N):
                    lam = y * wide[member, rows, columns(N + n)] + cs[n]
                    pulled = pulled + lam * wide[member, rows, columns(n)]
                    products.append(lam * d)
                    cs[n] = lam * jnp.exp2(s * table[2 + course, n])
                    at = pl.multiple_of((k * N + n) * CHUNKS, CHUNKS)
                    u = cs[n] * states[pl.ds(at, CHUNKS)]
                    slope = slope + u * table[course, n]
                    ds[n] = ds[n] + u * s
                slope_y[member, rows] = slope
                pull_y[member, rows] = pulled
                kept.append(products)
            pair = i if flipped else steps // 2 - 1 - i
            rows = pl.ds(pl.multiple_of(pair * 16, 16), 16)
            first, second = (kept[0], kept[1]) if flipped else (kept[1], kept[0])
            for n in range(N):
                both = low(jnp.concatenate([first[n], second[n]], axis=0))
                quads[rows, n * LANES : (n + 1) * LANES] = both
            return tuple(cs), tuple(ds)

        start = tuple(adjoint[member, n * CHUNKS : (n + 1) * CHUNKS] for n in range(N))
        zeros = (jnp.zeros((CHUNKS, LANES), F32),) * N
        _, ds = lax.fori_loop(0, steps // 2, back, (start, zeros))
        for n in range(N):
            rows = slice(n * CHUNKS, (n + 1) * CHUNKS)
            dacc[course, rows] = dacc[course, rows] + ds[n]
        for part in range(2):
            rows = slice(R + part * N, R + (part + 1) * N)
            lanes = slice(part * N * LANES, (part + 1) * N * LANES)
            for at in range(0, tok, LANES):
                dproj[member, rows, at : at + LANES] = nt(spread[rows, lanes], quads[at : at + LANES, lanes])

    lax.fori_loop(0, 2, lambda i, c: (sweep(3 * i, False), c)[1], 0)
    lax.fori_loop(0, 2, lambda i, c: (sweep(1 + i, True), c)[1], 0)

    small[...] = jnp.zeros_like(small)
    for course in range(2):
        for n in range(N):
            total = jnp.sum(dacc[course, n * CHUNKS : (n + 1) * CHUNKS], axis=0, keepdims=True)
            at = 2 * R + course * N + n
            small[at : at + 1] = total * table[course, n, :1]
    for strand in range(2):
        joined = jnp.zeros((tok, LANES), F32)
        grad = dys[strand]
        for course in range(2):
            member = 2 * strand + course
            active = act[member].astype(F32)
            joined = joined + out_y[member] + tiny[12 + course : 13 + course] * active
            raw_grad = slope_y[member] + pull_y[member] * active
            rounded = low(raw_grad * valid[...] * sigmoid(raw[member]))
            dact[member] = pull_y[member] * step[member] + grad * tiny[12 + course : 13 + course]
            rows = slice(course * R, (course + 1) * R)
            small[rows] += nn(proj[member, :R], rounded)
            at = 2 * R + 2 * N + course
            small[at : at + 1] += jnp.sum(rounded.astype(F32), axis=0, keepdims=True)
            small[at + 2 : at + 3] += jnp.sum(grad * active, axis=0, keepdims=True)
            at = COLUMNS * course
            message[strand, at : at + R] = low(nt(stw[course], rounded))
            message[strand, at + R : at + COLUMNS] = low(dproj[member, R:])
        gate = gates[strand]
        mixed[strand] = low(joined * silu(gate) * valid[...])
        dgate[strand] = low(gm[strand] * joined * silu_slope(gate))


E_ROWS = 608
L_ROWS = 384
GAIN_ROWS = 16


def halves(pack, total, keep, send):
    half = total // 2
    mine = lax.rem(lax.axis_index("rows"), 2)
    if keep.shape[0] >= total:
        keep[:total] = pack[:total]
        send[:half] = jnp.zeros((half, LANES), BF16)
    else:
        keep[:half] = pack[pl.ds(pl.multiple_of(mine * half, 16), half)]
        send[:half] = low(pack[pl.ds(pl.multiple_of((1 - mine) * half, 16), half)])


def dense_kernel(
    geo, mixed, outs, moved, dgate, normed, weights, back, small, kept, sent, keep, send, g_gate, dn_gate, pack
):
    width = weights.shape[1]
    second = lax.axis_index("ch") >= 2
    branches = []
    grad_out = jnp.zeros((LANES, width), F32)
    grad_gate = jnp.zeros(g_gate.shape, F32)
    for strand in range(2):
        branches.append(nn(low(nn(back[...], mixed[strand])), outs[strand]))
        grad_out = grad_out + tn(mixed[strand], moved[strand])
        grad_gate = grad_gate + tn(normed[strand], dgate[strand])
        dn_gate[strand] = nt(low(nn(back[...], dgate[strand])), weights[1 + 2 * strand])
    kept[...] = jnp.where(second, branches[1], branches[0])
    sent[...] = low(jnp.where(second, branches[0], branches[1]))
    g_gate[...] = grad_gate
    pack[:width] = grad_gate
    pack[width : width + LANES] = grad_out[:, :LANES]
    pack[width + LANES : width + 2 * LANES] = grad_out[:, LANES:]
    pack[width + 2 * LANES : width + 2 * LANES + 80] = small[...]
    pack[width + 2 * LANES + 80 :] = jnp.zeros((16, LANES), F32)
    halves(pack, E_ROWS, keep, send)


def conv_back_kernel(
    geo, one, two, act, dact, pre, padded, tiny, select, normed, rims_normed, gains, w, g_gate, valid, edge,
    xg, near, far, keep, send, gain_rows,
    pad_grad, pack,
):
    tok, steps = geo.tok, geo.steps
    taps = (padded.shape[1] // CHUNKS - steps) // 2 + 1
    width = w.shape[1]
    even = lax.rem(lax.axis_index("rows"), 2) == 0
    rim = taps - 1
    sub = iota((CHUNKS, LANES), 0)
    pack[...] = jnp.zeros_like(pack)
    grad_select = [jnp.zeros((COLUMNS, LANES), F32)] * 2
    grad_in = jnp.zeros((width, LANES), F32)
    at_conv = width + LANES - 32
    for strand in range(2):
        pad_grad[...] = jnp.zeros_like(pad_grad)
        rounded = low(one[strand].astype(F32) + two[strand].astype(F32))
        for course in range(2):
            member = 2 * strand + course
            mine = slice(COLUMNS * course, COLUMNS * (course + 1))
            grad_select[course] = grad_select[course] + nn(rounded[mine], act[member])
            total = dact[member] + tn(rounded[mine], select[course])
            grad = total * silu_slope(pre[member])
            row = at_conv + 8 + course
            pack[row : row + 1] += jnp.sum(grad, axis=0, keepdims=True)
            for tap in range(taps):
                at = tap_start(tap, taps, FLIPS[member])
                row = at_conv + course * taps + tap
                pack[row : row + 1] += jnp.sum(grad * padded[strand, at : at + tok], axis=0, keepdims=True)
                at_tap = course * taps + tap
                pad_grad[at : at + tok] += tiny[at_tap : at_tap + 1] * grad
        before = [jnp.zeros((1, LANES), F32)] * (16 - rim)
        after = []
        for k in range(rim, 0, -1):
            block = pad_grad[(rim - k) * CHUNKS : (rim - k + 1) * CHUNKS]
            before.append(block[:1])
            moved = jnp.where(sub == CHUNKS - 1, 0.0, pltpu.roll(block, CHUNKS - 1, 0))
            at = (rim + steps - k) * CHUNKS
            pad_grad[at : at + CHUNKS] += moved
        for k in range(rim):
            at = (rim + steps + k) * CHUNKS
            block = pad_grad[at : at + CHUNKS]
            after.append(block[CHUNKS - 1 :])
            moved = jnp.where(sub == 0, 0.0, pltpu.roll(block, 1, 0))
            at = (rim + k) * CHUNKS
            pad_grad[at : at + CHUNKS] += moved
        after += [jnp.zeros((1, LANES), F32)] * (16 - rim)
        rims = jnp.concatenate(before + after, axis=0) * edge[...]
        main = pad_grad[rim * CHUNKS : (rim + steps) * CHUNKS]
        xg[strand] = main
        grad_in = grad_in + tn(normed[strand], low(main * valid[...])) + tn(rims_normed[strand], low(rims))
        near[strand] = jnp.where(even, rims[16:], rims[:16])
        far[strand] = jnp.where(even, rims[:16], rims[16:])
    pack[:width] = grad_in
    for course in range(2):
        pack[width + course * COLUMNS : width + (course + 1) * COLUMNS] = grad_select[course]
    halves(pack, L_ROWS, keep, send)
    product = grad_in * w[0].astype(F32) + g_gate[...] * w[1].astype(F32)
    high = low(product)
    ones = jnp.ones((8, LANES), BF16)
    gain_part = (nt(ones, high) + nt(ones, low(product - high.astype(F32)))) / gains[:1]
    gain_rows[:8] = gain_part[:, :LANES]
    gain_rows[8:] = gain_part[:, LANES:]


def normed_back_kernel(
    geo, xg, near, far, dn_gate, weights, valid, back, kept, sent
):
    tok, steps = geo.tok, geo.steps
    even = lax.rem(lax.axis_index("rows"), 2) == 0
    second = lax.axis_index("ch") >= 2
    row = iota((tok, LANES), 0)
    token = (row % CHUNKS) * steps + row // CHUNKS
    grads = []
    for strand in range(2):
        one, two = near[strand], far[strand]
        ahead = jnp.where(even, two, one)
        behind = jnp.where(even, one, two)
        total = xg[strand]
        for k in range(3):
            total = total + jnp.where(token == k, ahead[k : k + 1], 0.0)
            total = total + jnp.where(token == tok - 1 - k, behind[15 - k : 16 - k], 0.0)
        rounded = low(total * valid[...])
        grads.append(nt(low(nn(back[...], rounded)), weights[2 * strand]) + dn_gate[strand])
    kept[...] = jnp.where(second, grads[1], grads[0])
    sent[...] = low(jnp.where(second, grads[0], grads[1]))


def finish_kernel(geo, one, two, xo, xc, gains, cot, res_own, res_got, input_grad, result):
    mine = lax.axis_index("ch")
    odd = lax.rem(mine, 2) == 1
    a, b = xo[...].astype(F32), xc[...].astype(F32)
    source = jnp.concatenate([jnp.where(odd, b, a), jnp.where(odd, a, b)], axis=1)
    inverse = lax.rsqrt(jnp.mean(source * source, axis=-1, keepdims=True) + EPSILON)
    unit = source * inverse
    here = jnp.where(mine >= 2, gains[1:], gains[:1])
    scaled = (one[...].astype(F32) + two[...].astype(F32)) * here
    back = inverse * (scaled - unit * jnp.mean(scaled * unit, axis=-1, keepdims=True))
    result[...] = low(xo[...].astype(F32) + res_own[...] + res_got[...].astype(F32))
    input_grad[...] = cot[...].astype(F32) + jnp.where(odd, back[:, LANES:], back[:, :LANES])


def unpack_kernel(e_parts, l_parts, in_g, out_g, sel_g, cw_g, cb_g, stw_g, stb_g, decay_g, skip_g, gain_g, e_pack, l_pack):
    mine = lax.rem(lax.axis_index("rows"), 2)
    for parts, pack in ((e_parts, e_pack), (l_parts, l_pack)):
        total = pack.shape[0]
        half = total // 2
        if len(parts) == 1:
            pack[...] = parts[0][:total].astype(F32)
        else:
            pack[pl.ds(pl.multiple_of(mine * half, 16), half)] = parts[0][:half].astype(F32)
            pack[pl.ds(pl.multiple_of((1 - mine) * half, 16), half)] = parts[1][:half].astype(F32)
    width = in_g.shape[1]
    in_g[0] = l_pack[:width]
    in_g[1] = e_pack[:width]
    out_g[:, :LANES] = e_pack[width : width + LANES]
    out_g[:, LANES:] = e_pack[width + LANES : width + 2 * LANES]
    amount = sel_g.shape[1]
    for course in range(2):
        sel_g[course] = l_pack[width + course * amount : width + (course + 1) * amount]
    at = width + 2 * amount
    taps = cw_g.shape[1]
    for course in range(2):
        cw_g[course] = l_pack[at + course * taps : at + (course + 1) * taps]
    cb_g[...] = l_pack[at + 2 * taps : at + 2 * taps + 2]
    at = width + 2 * LANES
    for course in range(2):
        stw_g[course] = e_pack[at + course * R : at + (course + 1) * R]
        decay_g[course] = e_pack[at + 2 * R + course * N : at + 2 * R + (course + 1) * N]
    at = at + 2 * R + 2 * N
    stb_g[...] = e_pack[at : at + 2]
    skip_g[...] = e_pack[at + 2 : at + 4]
    total = sum(part[part.shape[0] - GAIN_ROWS :].astype(F32) for part in l_parts)
    gain_g[:, :LANES] = total[:1]
    gain_g[:, LANES:] = total[8:9]


def swap(value, axis, distance):
    count = lax.axis_size(axis)
    return lax.ppermute(value, axis, [(i, i ^ distance) for i in range(count)])


def gather_channels(value):
    across = swap(value, "ch", 2)
    return value, swap(value, "ch", 1), across, swap(across, "ch", 1)


def partner_sum(value):
    joined = low(value.astype(F32) + swap(value, "ch", 2).astype(F32))
    return joined, swap(joined, "ch", 1)


def on_device(
    hidden_in, lengths, norm_gain, in_weight, conv_weight, conv_bias, select_weight,
    step_weight, step_bias, decay_log, skip_gain, out_weight, cotangent,
):
    tok = hidden_in.shape[0]
    rows = lax.axis_size("rows")
    geo = Geometry(tok, rows)
    steps = geo.steps
    width = in_weight.shape[1]
    gain = norm_gain[None, :]
    small_mesh = geo.members == 4 and rows == 8
    padded_rows = (steps + 2 * (conv_weight.shape[1] - 1)) * CHUNKS

    def kernel(f):
        return functools.partial(f, geo)

    def lifted(f, first, amount):
        def body(*refs):
            return f(*refs[:first], refs[first : first + amount], *refs[first + amount :])

        return body

    vm = pltpu.VMEM
    strands = ((2, tok, LANES), F32)
    strands_low = ((2, tok, LANES), BF16)
    members = ((4, tok, LANES), F32)
    members_low = ((4, tok, LANES), BF16)
    chunked = ((4, N * CHUNKS, LANES), F32)
    summary = ((5 * N, LANES), BF16)
    full = ((tok, width), F32)
    full_low = ((tok, width), BF16)

    x_parts = gather_channels(hidden_in)
    x_own, c_own, valid, edge, turn, mover, back, gains, weights, outs, select, table, spread, tiny, stw = run(
        kernel(prepare_kernel),
        [
            ((tok, LANES), BF16),
            ((tok, LANES), BF16),
            ((tok, LANES), F32),
            ((32, LANES), F32),
            ((width, width), BF16),
            ((tok, tok), BF16),
            ((tok, tok), BF16),
            ((2, width), F32),
            ((4, width, LANES), BF16),
            ((2, LANES, width), BF16),
            ((2, COLUMNS, LANES), BF16),
            ((4, N, CHUNKS, LANES), F32),
            ((2 * COLUMNS, 2 * N * LANES), BF16),
            ((24 + 2 * N, LANES), F32),
            (step_weight.shape, BF16),
        ],
        lengths, hidden_in, cotangent, in_weight, out_weight, step_weight, gain, conv_weight, conv_bias,
        jnp.swapaxes(select_weight, 1, 2), step_bias, decay_log, skip_gain,
        anywhere=13,
        scratch=[
            pltpu.SMEM(lengths.shape, jnp.int32),
            vm(gain.shape, F32),
            vm(conv_weight.shape, F32),
            vm(conv_bias.shape, F32),
            vm(step_bias.shape, F32),
            vm(decay_log.shape, F32),
            vm(skip_gain.shape, F32),
            pltpu.SemaphoreType.DMA((13,)),
        ],
        micros=2,
    )
    x_parts = (x_own,) + x_parts[1:]
    c_parts = (c_own,) + gather_channels(cotangent)[1:]

    normed, inputs, gates, near, far = run(
        kernel(project_kernel),
        [((2, tok, width), BF16), strands_low, strands, ((16, 2 * width), BF16), ((16, 2 * width), BF16)],
        *x_parts, valid, turn, mover, gains, weights,
        scratch=[vm((4, tok, LANES), BF16)],
    )
    near = lax.ppermute(near, "rows", geo.near())
    far = lax.ppermute(far, "rows", geo.far())
    moved, gm, dys = run(
        kernel(cotangent_kernel),
        [((2, tok, width), BF16), strands, strands],
        *c_parts, gates, valid, turn, mover, outs,
        scratch=[vm((4, tok, LANES), BF16)], micros=1,
    )
    padded, rims_normed, pre, act, message = run(
        kernel(conv_kernel),
        [((2, padded_rows, LANES), F32), ((2, 32, width), BF16), members, members_low, ((2, 2 * COLUMNS, tok), BF16)],
        inputs, near, far, edge, turn, gains, weights, select, tiny, dys,
    )
    one, two = partner_sum(message)
    shapes = [((4, COLUMNS, tok), BF16), members, members, members, chunked, chunked, chunked]
    shapes += [((4, tok, 2 * N * LANES), F32)]

    got = run(
        functools.partial(summary_kernel, geo, small_mesh), shapes + [summary, summary],
        one, two, act, dys, stw, tiny, table, spread, valid,
        scratch=[vm(summary[0], F32), vm(summary[0], F32)], micros=6,
    )
    proj, raw, step, drive, chunk_p, chunk_h, chunk_w, wide = got[:8]
    if small_mesh:
        slots = (
            lax.ppermute(got[8], "rows", geo.near()),
            lax.ppermute(got[9], "rows", geo.across()),
            lax.ppermute(got[9], "rows", geo.far()),
        )
        slot_scratch = vm((4,) + summary[0], BF16)
    else:
        up, down = lax.all_gather(got[8], "rows"), lax.all_gather(got[9], "rows")
        place = lax.axis_index("rows")
        index = place - geo.local() + jnp.arange(geo.members)
        inside = jnp.clip(index, 0, rows - 1)
        slots = (jnp.where((index < place)[:, None, None], up[inside], down[inside]),)
        slot_scratch = vm((16, LANES), BF16)
    mixed, dgate, dact, message, small = run(
        lifted(kernel(scan_kernel), 0, len(slots)),
        [strands_low, strands_low, members, ((2, 2 * COLUMNS, tok), BF16), ((80, LANES), F32)],
        *slots, act, proj, raw, step, drive, chunk_p, chunk_h, chunk_w, wide, spread,
        dys, gm, gates, stw, tiny, table, valid,
        scratch=[
            slot_scratch,
            vm(chunked[0], F32),
            vm(chunked[0], F32),
            vm(((steps + 1) * N * CHUNKS, LANES), F32),
            vm((tok, 2 * N * LANES), BF16),
            vm(members[0], F32),
            vm(members[0], F32),
            vm(members[0], F32),
            vm((4, COLUMNS, tok), F32),
            vm((2, N * CHUNKS, LANES), F32),
        ],
        micros=16, limit=14,
    )
    one, two = partner_sum(message)
    e_half = E_ROWS // 2
    l_half = L_ROWS // 2
    res_kept, res_sent, e_keep, e_send, g_gate, dn_gate = run(
        kernel(dense_kernel),
        [
            full,
            full_low,
            ((e_half if small_mesh else E_ROWS, LANES), F32),
            ((e_half, LANES), BF16),
            ((width, LANES), F32),
            ((2, tok, width), F32),
        ],
        mixed, outs, moved, dgate, normed, weights, back, small,
        scratch=[vm((E_ROWS, LANES), F32)],
    )
    res_got = swap(res_sent, "ch", 2)
    if small_mesh:
        e_sum = low(e_keep + swap(e_send, "rows", 1).astype(F32))
    xg, near, far, l_keep, l_send, gain_part = run(
        kernel(conv_back_kernel),
        [
            strands,
            ((2, 16, LANES), F32),
            ((2, 16, LANES), F32),
            ((l_half if small_mesh else L_ROWS, LANES), F32),
            ((l_half, LANES), BF16),
            ((GAIN_ROWS, LANES), F32),
        ],
        one, two, act, dact, pre, padded, tiny, select, normed, rims_normed, gains, weights, g_gate, valid, edge,
        scratch=[vm((padded_rows, LANES), F32), vm((L_ROWS, LANES), F32)],
    )
    near = lax.ppermute(near, "rows", geo.near())
    if small_mesh:
        gain_part = gain_part + swap(gain_part, "ch", 2)
        gain_part = gain_part + swap(gain_part, "ch", 1)
        l_sum = jnp.concatenate([l_keep + swap(l_send, "rows", 1).astype(F32), gain_part], axis=0)
        e_sum = low(e_sum.astype(F32) + swap(e_sum, "rows", 2).astype(F32))
        e_sum = low(e_sum.astype(F32) + swap(e_sum, "rows", 4).astype(F32))
    far = lax.ppermute(far, "rows", geo.far())
    total = res_kept + res_got.astype(F32)
    odd = lax.axis_index("ch") % 2 == 1
    res_own = jnp.where(odd, total[:, LANES:], total[:, :LANES])
    res_got = swap(low(jnp.where(odd, total[:, :LANES], total[:, LANES:])), "ch", 1)
    dn_kept, dn_sent = run(
        kernel(normed_back_kernel),
        [full, full_low],
        xg, near, far, dn_gate, weights, valid, back,
    )
    dn_got = swap(dn_sent, "ch", 2)
    dn = low(dn_kept + dn_got.astype(F32))
    input_grad, result = run(
        kernel(finish_kernel), [((tok, LANES), F32), ((tok, LANES), BF16)],
        dn, swap(dn, "ch", 1), x_parts[0], x_parts[1], gains, c_own, res_own, res_got,
    )
    if small_mesh:
        l_sum = low(l_sum + swap(low(l_sum), "rows", 2).astype(F32))
        l_sum = low(l_sum.astype(F32) + swap(l_sum, "rows", 4).astype(F32))
        e_parts = (e_sum, swap(e_sum, "rows", 1))
        l_parts = (l_sum, swap(l_sum, "rows", 1))
    else:
        e_parts = (lax.psum(e_keep, "rows"),)
        gain_part = lax.psum(gain_part, ("rows", "ch"))
        l_parts = (jnp.concatenate([lax.psum(l_keep, "rows"), gain_part], axis=0),)

    def unpack(*refs):
        k = len(e_parts)
        unpack_kernel(refs[:k], refs[k : 2 * k], *refs[2 * k :])

    got = run(
        unpack,
        [
            (in_weight.shape, F32),
            (out_weight.shape, F32),
            (jnp.swapaxes(select_weight, 1, 2).shape, F32),
            (conv_weight.shape, F32),
            (conv_bias.shape, F32),
            (step_weight.shape, F32),
            (step_bias.shape, F32),
            (decay_log.shape, F32),
            (skip_gain.shape, F32),
            ((1, width), F32),
        ],
        *e_parts, *l_parts,
        scratch=[vm((E_ROWS, LANES), F32), vm((L_ROWS, LANES), F32)],
    )
    in_g, out_g, sel_g, cw_g, cb_g, stw_g, stb_g, decay_g, skip_g, gain_g = got
    return (
        result, input_grad, gain_g[0], in_g, cw_g, cb_g, jnp.swapaxes(sel_g, 1, 2), stw_g, stb_g, decay_g, skip_g, out_g,
    )


def solution(mesh):
    lanes = P(None, None, "ch")
    pair = P(None, "ch")
    columns = P(None, "ch", None)
    tokens = P("rows", "ch")
    return jax.shard_map(
        on_device,
        mesh=mesh,
        in_specs=(
            tokens, P(), P(), lanes, lanes, pair, columns, lanes, pair, lanes, pair, P("ch", None), tokens,
        ),
        out_specs=(
            tokens, tokens, P(), lanes, lanes, pair, columns, lanes, pair, lanes, pair, P("ch", None),
        ),
        check_vma=False,
    )
```
